256 devices in a mesh: real: 16 (over x_hi, y, core), site: 16 (over x_lo, z).
Axes of the slice: x: 4 (x_hi: 2, x_lo: 2; x = x_hi * 2 + x_lo), y: 4, z: 8, core: 2. Of those that a mesh axis runs over, the one named last changes fastest.
Arguments:
- noise: bfloat16 [16384, 12288], P('site', 'real'), may hold values from -6 to 6
- v_factors: bfloat16 [16, 1024, 4096], P('site', 'real'), may hold values from -0.1875 to 0.1875
- u_factors: bfloat16 [16, 1024, 4096], P('site', 'real'), may hold values from -0.09375 to 0.09375
- ranks: int32 [16, 16], replicated, may hold values from 1 to 2, as said below
- skew_g: float32 [16384], P('site'), may hold values from 0.1 to 0.6
- tail_h: float32 [16384], P('site'), may hold values from 0.05 to 0.3
Outputs:
- field: float32 [16384, 12288], P('site', 'real')
The draws below stay inside these ranges and needn't reach their ends.
Inputs may be any that keep to these rules, and one draw needn't show every extreme that they name: `ranks`: every tile has at least one rank block, and some tile has 2.
All inputs are finite; a program needn't handle non-finite values.
Results may differ from the reference program's by a relative error of at most 0.012.
The reference program's roundings to bfloat16 on the way (of `coef`) count: a program that leaves them out, or rounds other values in their place, can miss the bound.
Values may be sent and summed in bfloat16 or wider, within the bound.
A program may use at most 128 MiB of HBM per device.

```python
import math
import jax
import jax.numpy as jnp
from jax import lax

TILE = 1024
RANKB = 128
CAP = 2
SITES = 16384
REALS = 12288
RANK_COLS = 4096
N_SITE = 16


def draw_ranks(key, part):
    first_key, second_key = jax.random.split(jax.random.fold_in(key, 11))
    base = jax.random.randint(first_key, (N_SITE * N_SITE,), 1, CAP + 1)
    chosen = jax.random.randint(second_key, (), 0, N_SITE * N_SITE)
    filled = jnp.where(jnp.arange(N_SITE * N_SITE) == chosen, CAP, base)
    return filled.reshape(N_SITE, N_SITE).astype(jnp.int32)


def steps_of(rng, shape, pieces, least, top_value):
    loudness, own = 1.0, jax.random.fold_in(rng, 6)
    for axis_at, shards_of in pieces:
        draws = jnp.exp(jax.random.uniform(jax.random.fold_in(own, axis_at), (shards_of,), jnp.float32, least / len(pieces), top_value / len(pieces)))
        loudness = loudness * jnp.repeat(draws, shape[axis_at] // shards_of).reshape([-1 if axis == axis_at else 1 for axis in range(len(shape))])
    return loudness


def bell_draw(key, dims, spread, limit, shards=(), kind=jnp.bfloat16):
    values = jax.random.normal(key, dims, jnp.float32) * spread
    if len(shards) > 0:
        values = steps_of(key, dims, shards, -0.22, 0.18) * values
    return jnp.clip(values, min=-limit, max=limit).astype(kind)


def setup_inputs(seed: int = 0) -> dict:
    key_of = jax.random.split(jax.random.key(seed), 7)
    return {
        "noise": bell_draw(key_of[0], (SITES, REALS), 1.0, 6.0, ((0, 16), (1, 16))),
        "v_factors": bell_draw(key_of[1], (N_SITE, TILE, RANK_COLS), TILE ** -0.5, 0.1875, ((0, 16), (1, 16))),
        "u_factors": bell_draw(key_of[2], (N_SITE, TILE, RANK_COLS), RANK_COLS ** -0.5, 0.09375, ((0, 16), (1, 16))),
        "ranks": draw_ranks(jax.random.fold_in(key_of[6], 71), 0),
        "skew_g": jnp.clip(jnp.exp(math.log(0.6) - 1.7917595 * jax.random.uniform(key_of[4], (SITES,), jnp.float32) ** steps_of(key_of[4], (SITES,), ((0, 16),), -0.2, 0.2)), 0.1, 0.6),
        "tail_h": jnp.clip(0.05 + 0.25 * jax.random.uniform(key_of[5], (SITES,), jnp.float32) ** steps_of(key_of[5], (SITES,), ((0, 16),), -0.2, 0.2), 0.05, 0.3),
    }


def reference(noise, v_factors, u_factors, ranks, skew_g, tail_h):
    per_tile = CAP * RANKB
    levels = jnp.arange(CAP, dtype=jnp.int32)
    alive = (levels[None, None, :] < jnp.transpose(ranks)[:, :, None]).astype(jnp.float32)
    noise_tiles = noise.reshape(N_SITE, TILE, -1)
    u_by_source = jnp.transpose(u_factors.reshape(N_SITE, TILE, N_SITE, per_tile), (2, 0, 1, 3))

    def add_source(running, inputs):
        v_tile, noise_tile, alive_col, u_tiles = inputs
        projected = lax.dot_general(v_tile, noise_tile, (((0,), (0,)), ((), ())), preferred_element_type=jnp.float32)
        masked = projected.reshape(N_SITE, CAP, RANKB, -1) * alive_col[:, :, None, None]
        coef = masked.astype(jnp.bfloat16).reshape(N_SITE, per_tile, -1)
        contrib = jnp.einsum("itr,irn->itn", u_tiles.astype(jnp.float32), coef.astype(jnp.float32),
                             precision=lax.Precision.HIGHEST)
        return running + contrib.reshape(N_SITE * TILE, -1), None

    start_sum = jnp.zeros((N_SITE * TILE, noise.shape[1]), jnp.float32)
    gaussian, _ = lax.scan(add_source, start_sum, (v_factors, noise_tiles, alive, u_by_source))
    skew_col = skew_g[:, None]
    tail_col = tail_h[:, None]
    return jnp.expm1(skew_col * gaussian) / skew_col * jnp.exp(0.5 * tail_col * gaussian * gaussian)
```

```python
import functools

import jax
import jax.numpy as jnp
from jax import lax
from jax.experimental import pallas as pl
from jax.experimental.pallas import tpu as pltpu
from jax.sharding import PartitionSpec as P

MESH = pl.DeviceIdType.MESH
CAP = 2
ZS = 8
YS = 4
CHUNKS = 3

SLOTS = (
    (0, 1, 0), (1, 1, 0), (-1, 1, 0), (2, 1, 0), (-2, 1, 0),
    (-2, 0, 1), (-2, 1, 1), (2, 0, -1),
    (2, 1, -1), (-2, 0, 2), (2, 1, -2),
    (0, 0, 0), (1, 0, 0), (-1, 0, 0), (2, 0, 0), (-2, 0, 0),
)
SENT = 11
EARLY = ((0, 5), (11, 16))
LATE = (5, 11)
AT = {0: 0, 1: 1, -1: 2, 2: 3, -2: 4}
HALVES = 2


def tukey(x, g, h):
    y = g * x
    series = y * (1.0 + y * (0.5 + y * (1.0 / 6 + y * (1.0 / 24 + y * (1.0 / 120 + y * (1.0 / 720 + y * (1.0 / 5040)))))))
    lifted = jnp.where(jnp.abs(y) < 0.35, series, jnp.exp(y) - 1.0)
    return lifted / g * jnp.exp(0.5 * h * x * x)


def kernel(noise, v, u, ranks, skew, tail, out, nt, gv, gu, cs, cr, gb, hb, vs, vr, as_, ar, ns, nr, ps, pr, local):
    real, site = lax.axis_index("real"), lax.axis_index("site")
    core = lax.rem(real, 2)
    y = lax.rem(lax.div(real, 2), YS)
    xh = lax.div(real, 2 * YS)
    x = lax.div(site, ZS)
    z = lax.rem(site, ZS)
    rows = v.shape[0]
    unit = v.shape[1] // len(SLOTS)
    rank_block = unit // CAP
    piece = noise.shape[1] // CHUNKS

    def site_of(fx, dz):
        return (1 - x if fx else x) * ZS + lax.rem(z + dz + ZS, ZS)

    def real_of(fh, dy, fc):
        hi = 1 - xh if fh else xh
        lo = 1 - core if fc else core
        return (hi * YS + lax.rem(y + dy + YS, YS)) * 2 + lo

    def cols(index):
        return pl.ds(pl.multiple_of(index * unit, unit), unit)

    def fixed(index):
        return pl.ds(index * unit, unit)

    def part(c):
        return pl.ds(c * piece, piece)

    barrier = pltpu.get_barrier_semaphore()
    peers = [(real, site_of(0, d)) for d in (1, -1, 2, -2)]
    peers += [(real, site_of(1, d)) for d in (0, 1, -1, 2, -2)]
    peers += [(real_of(*w), site) for w in ((1, 0, 0), (0, 1, 0), (0, -1, 0), (0, 0, 1))]
    for peer in peers:
        pl.semaphore_signal(barrier, inc=1, device_id=peer, device_id_type=MESH)
    pl.semaphore_wait(barrier, len(peers))

    mine = pl.ds(pl.multiple_of(real * rows, rows), rows)

    def v_copy(m):
        dj, fx, di = SLOTS[m]
        wanted = cols(site_of(fx, di - dj))
        if dj == 0:
            return pltpu.make_async_copy(v.at[:, wanted], gv.at[mine, fixed(m)], local.at[m])
        return pltpu.make_async_remote_copy(
            src_ref=v.at[:, wanted], dst_ref=gv.at[mine, fixed(m)], send_sem=vs.at[m], recv_sem=vr.at[m],
            device_id=(real, site_of(0, -dj)), device_id_type=MESH,
        )

    v_copies = [v_copy(m) for m in range(len(SLOTS))]
    for copy in v_copies:
        copy.start()

    u_copies = []
    for m, (dj, fx, di) in enumerate(SLOTS):
        u_copies.append(
            pltpu.make_async_copy(u.at[:, cols(site_of(fx, dj - di))], gu.at[mine, fixed(m)], local.at[len(SLOTS) + m])
        )
        u_copies[-1].start()

    KINDS = (
        ((0, 0), (1, 0, 0)),
        ((0, 0), (0, 1, 0)), ((0, 0), (0, -1, 0)),
        ((1, 0), (0, 1, 0)), ((1, 0), (0, -1, 0)),
        ((0, -1), (0, 1, 0)), ((1, 1), (0, -1, 0)),
    ) + tuple((block, (0, 0, 1)) for block in ((0, 0), (1, 0), (0, -1), (0, 1), (1, -1), (1, 1), (0, 2), (1, 2)))

    def gather(buffer, which, half):
        width = buffer.shape[1] // HALVES
        copies = []
        for kind, ((fh, dy), to) in enumerate(KINDS):
            owner = real_of(fh, dy, 0)
            block = buffer.at[pl.ds(pl.multiple_of(owner * rows, rows), rows), pl.ds(half * width, width)]
            index = (which * HALVES + half) * len(KINDS) + kind
            copies.append(
                pltpu.make_async_remote_copy(
                    src_ref=block, dst_ref=block, send_sem=as_.at[index], recv_sem=ar.at[index],
                    device_id=(real_of(*to), site), device_id_type=MESH,
                )
            )
        return copies

    def start(copies, *kinds):
        for kind in kinds:
            copies[kind].start()

    def step(copies, number):
        if number == 0:
            start(copies, 0, 1, 2, 7)
        elif number == 1:
            copies[0].wait_recv()
            start(copies, 3, 4, 8)
        elif number == 2:
            copies[1].wait_recv()
            start(copies, 5, 9)
            copies[2].wait_recv()
            start(copies, 10)
        elif number == 3:
            copies[4].wait_recv()
            start(copies, 6, 12)
            copies[3].wait_recv()
            start(copies, 11)
        elif number == 4:
            copies[5].wait_recv()
            start(copies, 13)
            copies[6].wait_recv()
            start(copies, 14)
        else:
            for kind in range(7, 15):
                copies[kind].wait_recv()

    va, vb = gather(gv, 0, 0), gather(gv, 0, 1)
    ua, ub = gather(gu, 1, 0), gather(gu, 1, 1)

    def noise_copy(c, way, hop):
        return pltpu.make_async_remote_copy(
            src_ref=nt.at[0 if hop == 0 else AT[-way], part(c)],
            dst_ref=nt.at[AT[-way * (hop + 1)], part(c)],
            send_sem=ns.at[(c * 2 + (way > 0)) * 2 + hop], recv_sem=nr.at[(c * 2 + (way > 0)) * 2 + hop],
            device_id=(real, site_of(0, way)), device_id_type=MESH,
        )

    noise_copies = {(c, way, hop): noise_copy(c, way, hop) for c in range(CHUNKS) for way in (1, -1) for hop in (0, 1)}

    def turn(c):
        nt[0, part(c), :] = noise[:, part(c)].T

    def first(c):
        for way in (1, -1):
            noise_copies[c, way, 0].start()

    def forward(c):
        for way in (1, -1):
            noise_copies[c, way, 0].wait_recv()
            noise_copies[c, way, 1].start()

    def far(c):
        for way in (1, -1):
            noise_copies[c, way, 1].wait_recv()

    turn(0)
    turn(1)
    first(0)
    turn(2)
    first(1)

    for copy in u_copies:
        copy.wait()
    step(ua, 0)

    for m in range(len(SLOTS)):
        if SLOTS[m][0] == 0:
            v_copies[m].wait()
        else:
            v_copies[m].wait_recv()
        if m == len(SLOTS) // HALVES - 1:
            step(va, 0)
    step(vb, 0)

    for k in range(skew.shape[0]):
        spread = pl.ds(k * 128, 128)
        gb[spread, :] = jnp.broadcast_to(skew[pl.ds(k, 1), :], (128, 128)).T
        hb[spread, :] = jnp.broadcast_to(tail[pl.ds(k, 1), :], (128, 128)).T

    def coef_copy(m, c):
        dj, fx, di = SLOTS[m]
        return pltpu.make_async_remote_copy(
            src_ref=cs.at[part(c), fixed(m)], dst_ref=cr.at[part(c), fixed(m)],
            send_sem=ps.at[m * CHUNKS + c], recv_sem=pr.at[m * CHUNKS + c],
            device_id=(real, site_of(fx, di)), device_id_type=MESH,
        )

    coef_copies = {(m, c): coef_copy(m, c) for m in range(SENT) for c in range(CHUNKS)}
    level = lax.broadcasted_iota(jnp.int32, (1, unit), 1) // rank_block

    def project(m, c):
        dj, fx, di = SLOTS[m]
        projected = jnp.dot(nt[AT[dj], part(c), :], gv[:, fixed(m)], preferred_element_type=jnp.float32)
        alive = (level < ranks[site_of(fx, di), site_of(0, dj)]).astype(jnp.float32)
        (cs if m < SENT else cr)[part(c), fixed(m)] = (projected * alive).astype(jnp.bfloat16)

    def projects(*tasks):
        waiting = None
        for task in tasks:
            project(*task)
            if waiting is not None:
                coef_copies[waiting].start()
            waiting = task if task[0] < SENT else None
        if waiting is not None:
            coef_copies[waiting].start()

    def dot_t(left, right):
        return lax.dot_general(left, right, (((1,), (1,)), ((), ())), preferred_element_type=jnp.float32)

    block = 256

    def early(c):
        @pl.loop(0, out.shape[0] // block)
        def _(k):
            here = pl.ds(pl.multiple_of(k * block, block), block)
            total = None
            for lo, hi in EARLY:
                span = pl.ds(lo * unit, (hi - lo) * unit)
                term = dot_t(gu[here, span], cr[part(c), span])
                total = term if total is None else total + term
            out[here, part(c)] = total

    def late(c):
        @pl.loop(0, out.shape[0] // block)
        def _(k):
            here = pl.ds(pl.multiple_of(k * block, block), block)
            span = pl.ds(LATE[0] * unit, (LATE[1] - LATE[0]) * unit)
            total = out[here, part(c)] + dot_t(gu[here, span], cr[part(c), span])
            g, h = gb[here, :], hb[here, :]
            for q in range(piece // 128):
                out[here, pl.ds(c * piece + q * 128, 128)] = tukey(total[:, q * 128:(q + 1) * 128], g, h)

    def arrived(slots, c):
        for m in slots:
            coef_copies[m, c].wait_recv()

    step(va, 1)
    step(va, 2)
    forward(0)
    first(2)
    step(vb, 1)
    step(va, 3)
    step(vb, 2)
    step(va, 4)
    step(va, 5)
    projects((0, 0), (0, 1), (0, 2))
    forward(1)
    projects((1, 0), (2, 0), (1, 1), (2, 1))
    step(vb, 3)
    step(ua, 1)
    step(ub, 0)
    step(vb, 4)
    step(vb, 5)
    step(ua, 2)
    far(0)
    projects((5, 0), (6, 0), (7, 0), (8, 0), (9, 0), (10, 0), (3, 0), (4, 0))
    step(ub, 1)
    projects((11, 0), (12, 0), (13, 0), (14, 0), (15, 0))
    step(ua, 3)
    projects((11, 1), (12, 1), (13, 1), (11, 2))
    forward(2)
    projects((1, 2), (2, 2), (12, 2), (13, 2))
    step(ub, 2)
    step(ua, 4)
    far(1)
    projects((5, 1), (6, 1), (7, 1), (8, 1), (9, 1), (10, 1), (3, 1), (4, 1), (14, 1), (15, 1))
    step(ub, 3)
    step(ub, 4)
    step(ua, 5)
    step(ub, 5)
    arrived(range(5), 0)
    early(0)
    arrived(range(5, SENT), 0)
    late(0)
    far(2)
    projects((5, 2), (6, 2), (7, 2), (8, 2), (9, 2), (10, 2), (3, 2), (4, 2), (14, 2), (15, 2))
    arrived(range(5), 1)
    early(1)
    arrived(range(5, SENT), 1)
    late(1)
    arrived(range(5), 2)
    early(2)
    arrived(range(5, SENT), 2)
    late(2)

    for m, copy in enumerate(v_copies):
        if SLOTS[m][0] != 0:
            copy.wait_send()
    for copies in (va, vb, ua, ub):
        for copy in copies:
            copy.wait_send()
    for copy in noise_copies.values():
        copy.wait_send()
    for copy in coef_copies.values():
        copy.wait_send()


def per_device(noise, v_factors, u_factors, ranks, skew_g, tail_h):
    v, u = v_factors[0], u_factors[0]
    tile, count = noise.shape
    columns = v.shape[1]
    vmem = pl.BlockSpec(memory_space=pltpu.VMEM)
    dma = pltpu.SemaphoreType.DMA
    gathers = 2 * HALVES * 15
    return pl.pallas_call(
        kernel,
        out_shape=jax.ShapeDtypeStruct((tile, count), jnp.float32),
        in_specs=[vmem, vmem, vmem, pl.BlockSpec(memory_space=pltpu.SMEM), vmem, vmem],
        out_specs=vmem,
        scratch_shapes=[
            pltpu.VMEM((5, count, tile), jnp.bfloat16),
            pltpu.VMEM((tile, columns), jnp.bfloat16),
            pltpu.VMEM((tile, columns), jnp.bfloat16),
            pltpu.VMEM((count, columns // len(SLOTS) * SENT), jnp.bfloat16),
            pltpu.VMEM((count, columns), jnp.bfloat16),
            pltpu.VMEM((tile, 128), jnp.float32),
            pltpu.VMEM((tile, 128), jnp.float32),
            dma((16,)), dma((16,)),
            dma((gathers,)), dma((gathers,)),
            dma((4 * CHUNKS,)), dma((4 * CHUNKS,)),
            dma((SENT * CHUNKS,)), dma((SENT * CHUNKS,)),
            dma((32,)),
        ],
        compiler_params=pltpu.CompilerParams(
            collective_id=0, has_side_effects=True, vmem_limit_bytes=60 * 1024 * 1024
        ),
    )(noise, v, u, ranks, skew_g.reshape(-1, 128), tail_h.reshape(-1, 128))


def solution(mesh):
    placed = (
        P("site", "real"),
        P("site", "real", None),
        P("site", "real", None),
        P(),
        P("site"),
        P("site"),
    )
    return jax.shard_map(
        per_device, mesh=mesh, in_specs=placed, out_specs=P("site", "real"), check_vma=False
    )
```

```python
import functools

import jax
import jax.numpy as jnp
from jax import lax
from jax.experimental import pallas as pl
from jax.experimental.pallas import tpu as pltpu
from jax.sharding import PartitionSpec as P

MESH = pl.DeviceIdType.MESH
CAP = 2
ZS = 8
YS = 4
CHUNKS = ((0, 256), (256, 384), (640, 128))

SLOTS = (
    (0, 1, 0), (1, 1, 0), (-1, 1, 0), (2, 1, 0), (-2, 1, 0),
    (-2, 0, 1), (-2, 1, 1), (2, 0, -1),
    (2, 1, -1), (-2, 0, 2), (2, 1, -2),
    (0, 0, 0), (1, 0, 0), (-1, 0, 0), (2, 0, 0), (-2, 0, 0),
)
SENT = 11
EARLY = ((0, 5), (11, 16))
LATE = (5, 11)
AT = {0: 0, 1: 1, -1: 2, 2: 3, -2: 4}
QUARTERS, HALVES = 4, 2


def tukey(x, g, h):
    y = g * x
    series = y * (1.0 + y * (0.5 + y * (1.0 / 6 + y * (1.0 / 24 + y * (1.0 / 120 + y * (1.0 / 720 + y * (1.0 / 5040)))))))
    lifted = jnp.where(jnp.abs(y) < 0.35, series, jnp.exp(y) - 1.0)
    return lifted / g * jnp.exp(0.5 * h * x * x)


def kernel(noise_hbm, v, u, ranks_hbm, skew_hbm, tail_hbm, out_hbm,
           noise, ranks, skew, tail, out, nt, gv, gu, cs, cr, gb, hb,
           vs, vr, as_, ar, ns, nr, ps, pr, local):
    real, site = lax.axis_index("real"), lax.axis_index("site")
    core = lax.rem(real, 2)
    y = lax.rem(lax.div(real, 2), YS)
    xh = lax.div(real, 2 * YS)
    x = lax.div(site, ZS)
    z = lax.rem(site, ZS)
    rows = v.shape[0]
    unit = v.shape[1] // len(SLOTS)
    rank_block = unit // CAP

    def site_of(fx, dz):
        return (1 - x if fx else x) * ZS + lax.rem(z + dz + ZS, ZS)

    def real_of(fh, dy, fc):
        hi = 1 - xh if fh else xh
        lo = 1 - core if fc else core
        return (hi * YS + lax.rem(y + dy + YS, YS)) * 2 + lo

    def cols(index):
        return pl.ds(pl.multiple_of(index * unit, unit), unit)

    def fixed(index):
        return pl.ds(index * unit, unit)

    def part(c):
        return pl.ds(*CHUNKS[c])

    barrier = pltpu.get_barrier_semaphore()
    peers = [(real, site_of(0, d)) for d in (1, -1, 2, -2)]
    peers += [(real, site_of(1, d)) for d in (0, 1, -1, 2, -2)]
    peers += [(real_of(*w), site) for w in ((1, 0, 0), (0, 1, 0), (0, -1, 0), (0, 0, 1))]
    for peer in peers:
        pl.semaphore_signal(barrier, inc=1, device_id=peer, device_id_type=MESH)

    mine = pl.ds(pl.multiple_of(real * rows, rows), rows)
    loads = []

    def load(source, target):
        loads.append(pltpu.make_async_copy(source, target, local.at[len(loads)]))
        loads[-1].start()

    for c in range(len(CHUNKS)):
        load(noise_hbm.at[:, part(c)], noise.at[:, part(c)])
    load(skew_hbm, skew)
    load(tail_hbm, tail)
    load(ranks_hbm, ranks)
    for m, (dj, fx, di) in enumerate(SLOTS):
        if dj == 0:
            load(v.at[:, cols(site_of(fx, di))], gv.at[mine, fixed(m)])
    for m, (dj, fx, di) in enumerate(SLOTS):
        load(u.at[:, cols(site_of(fx, dj - di))], gu.at[mine, fixed(m)])

    v_copies = {}
    for m, (dj, fx, di) in enumerate(SLOTS):
        if dj != 0:
            v_copies[m] = pltpu.make_async_remote_copy(
                src_ref=v.at[:, cols(site_of(fx, di - dj))], dst_ref=gv.at[mine, fixed(m)],
                send_sem=vs.at[m], recv_sem=vr.at[m],
                device_id=(real, site_of(0, -dj)), device_id_type=MESH,
            )

    KINDS = (
        ((0, 0), (1, 0, 0)),
        ((0, 0), (0, 1, 0)), ((0, 0), (0, -1, 0)),
        ((1, 0), (0, 1, 0)), ((1, 0), (0, -1, 0)),
        ((0, -1), (0, 1, 0)), ((1, 1), (0, -1, 0)),
    ) + tuple((block, (0, 0, 1)) for block in ((0, 0), (1, 0), (0, -1), (0, 1), (1, -1), (1, 1), (0, 2), (1, 2)))
    gathers = []

    def gather(buffer, pieces):
        width = buffer.shape[1] // pieces
        for p in range(pieces):
            copies = []
            for kind, ((fh, dy), to) in enumerate(KINDS):
                owner = real_of(fh, dy, 0)
                block = buffer.at[pl.ds(pl.multiple_of(owner * rows, rows), rows), pl.ds(p * width, width)]
                index = len(gathers) * len(KINDS) + kind
                copies.append(
                    pltpu.make_async_remote_copy(
                        src_ref=block, dst_ref=block, send_sem=as_.at[index], recv_sem=ar.at[index],
                        device_id=(real_of(*to), site), device_id_type=MESH,
                    )
                )
            gathers.append(copies)

    gather(gv, QUARTERS)
    gather(gu, HALVES)
    ua, ub = gathers[QUARTERS], gathers[QUARTERS + 1]

    def start(copies, *kinds):
        for kind in kinds:
            copies[kind].start()

    def step(copies, number):
        if number == 0:
            start(copies, 0, 1, 2, 7)
        elif number == 1:
            copies[0].wait_recv()
            start(copies, 3, 4, 8)
        elif number == 2:
            copies[1].wait_recv()
            start(copies, 5, 9)
            copies[2].wait_recv()
            start(copies, 10)
        elif number == 3:
            copies[4].wait_recv()
            start(copies, 6, 12)
            copies[3].wait_recv()
            start(copies, 11)
        elif number == 4:
            copies[5].wait_recv()
            start(copies, 13)
            copies[6].wait_recv()
            start(copies, 14)
        else:
            for kind in range(7, 15):
                copies[kind].wait_recv()

    def steps(*numbers):
        for quarter, number in numbers:
            step(gathers[quarter], number)

    def noise_copy(c, way, hop):
        return pltpu.make_async_remote_copy(
            src_ref=nt.at[0 if hop == 0 else AT[-way], part(c)],
            dst_ref=nt.at[AT[-way * (hop + 1)], part(c)],
            send_sem=ns.at[(c * 2 + (way > 0)) * 2 + hop], recv_sem=nr.at[(c * 2 + (way > 0)) * 2 + hop],
            device_id=(real, site_of(0, way)), device_id_type=MESH,
        )

    noise_copies = {(c, way, hop): noise_copy(c, way, hop) for c in range(len(CHUNKS)) for way in (1, -1) for hop in (0, 1)}

    def turn(c):
        loads[c].wait()
        nt[0, part(c), :] = noise[:, part(c)].T

    def first(c):
        for way in (1, -1):
            noise_copies[c, way, 0].start()

    def forward(c):
        for way in (1, -1):
            noise_copies[c, way, 0].wait_recv()
            noise_copies[c, way, 1].start()

    def far(c):
        for way in (1, -1):
            noise_copies[c, way, 1].wait_recv()

    def coef_copy(m, c):
        dj, fx, di = SLOTS[m]
        return pltpu.make_async_remote_copy(
            src_ref=cs.at[part(c), fixed(m)], dst_ref=cr.at[part(c), fixed(m)],
            send_sem=ps.at[m * len(CHUNKS) + c], recv_sem=pr.at[m * len(CHUNKS) + c],
            device_id=(real, site_of(fx, di)), device_id_type=MESH,
        )

    coef_copies = {(m, c): coef_copy(m, c) for m in range(SENT) for c in range(len(CHUNKS))}
    level = lax.broadcasted_iota(jnp.int32, (1, unit), 1) // rank_block

    def project(m, c):
        dj, fx, di = SLOTS[m]
        projected = jnp.dot(nt[AT[dj], part(c), :], gv[:, fixed(m)], preferred_element_type=jnp.float32)
        alive = (level < ranks[site_of(fx, di), site_of(0, dj)]).astype(jnp.float32)
        (cs if m < SENT else cr)[part(c), fixed(m)] = (projected * alive).astype(jnp.bfloat16)

    def projects(c, *slots):
        waiting = None
        for m in slots:
            project(m, c)
            if waiting is not None:
                coef_copies[waiting, c].start()
            waiting = m if m < SENT else None
        if waiting is not None:
            coef_copies[waiting, c].start()

    def dot_t(left, right):
        return lax.dot_general(left, right, (((1,), (1,)), ((), ())), preferred_element_type=jnp.float32)

    block = 256

    def early(c):
        @pl.loop(0, out.shape[0] // block)
        def _(k):
            here = pl.ds(pl.multiple_of(k * block, block), block)
            total = None
            for lo, hi in EARLY:
                span = pl.ds(lo * unit, (hi - lo) * unit)
                term = dot_t(gu[here, span], cr[part(c), span])
                total = term if total is None else total + term
            out[here, part(c)] = total

    def late(c):
        begin, width = CHUNKS[c]

        @pl.loop(0, out.shape[0] // block)
        def _(k):
            here = pl.ds(pl.multiple_of(k * block, block), block)
            span = pl.ds(LATE[0] * unit, (LATE[1] - LATE[0]) * unit)
            total = out[here, part(c)] + dot_t(gu[here, span], cr[part(c), span])
            g, h = gb[here, :], hb[here, :]
            for q in range(0, width, 128):
                out[here, pl.ds(begin + q, 128)] = tukey(total[:, q:q + 128], g, h)

    stores = [
        pltpu.make_async_copy(out.at[:, part(c)], out_hbm.at[:, part(c)], local.at[len(loads) + c])
        for c in range(len(CHUNKS))
    ]

    def arrived(slots, c):
        for m in slots:
            coef_copies[m, c].wait_recv()

    beside = range(5)
    relayed = range(5, SENT)
    turn(0)
    pl.semaphore_wait(barrier, len(peers))
    for m in v_copies:
        v_copies[m].start()
    turn(1)
    first(0)
    turn(2)
    first(1)
    for copy in loads[len(CHUNKS):]:
        copy.wait()
    start(ua, 0, 7)
    for k in range(skew.shape[0]):
        spread = pl.ds(k * 128, 128)
        gb[spread, :] = jnp.broadcast_to(skew[pl.ds(k, 1), :], (128, 128)).T
        hb[spread, :] = jnp.broadcast_to(tail[pl.ds(k, 1), :], (128, 128)).T

    def ready(quarter):
        count = len(SLOTS) // QUARTERS
        for m in range(quarter * count, (quarter + 1) * count):
            if m in v_copies:
                v_copies[m].wait_recv()
        step(gathers[quarter], 0)

    ready(0)
    steps((0, 1))
    ready(1)
    steps((0, 2), (1, 1))
    ready(2)
    steps((0, 3), (1, 2), (2, 1))
    ready(3)
    start(ub, 0, 7)
    steps((0, 4), (1, 3), (2, 2), (3, 1))
    forward(0)
    first(2)
    steps((0, 5))
    projects(0, 0)
    projects(1, 0)
    steps((1, 4), (2, 3), (3, 2))
    start(ua, 1, 2)
    projects(0, 1, 2)
    steps((1, 5), (2, 4), (3, 3))
    step(ua, 1)
    projects(2, 0)
    forward(1)
    projects(1, 1, 2)
    steps((2, 5), (3, 4))
    step(ua, 2)
    start(ub, 1, 2)
    steps((3, 5))
    far(0)
    projects(0, 9, 10, 5, 6, 7, 8, 3, 4)
    step(ua, 3)
    step(ub, 1)
    forward(2)
    projects(2, 1, 2)
    projects(0, 11, 12, 13, 14, 15)
    step(ua, 4)
    step(ub, 2)
    projects(1, 11, 12, 13)
    projects(2, 11, 12, 13)
    step(ub, 3)
    far(1)
    projects(1, 9, 10, 5, 6, 7, 8, 3, 4)
    step(ub, 4)
    projects(1, 14, 15)
    step(ua, 5)
    step(ub, 5)
    arrived(beside, 0)
    early(0)
    far(2)
    projects(2, 9, 10, 5, 6, 7, 8, 3, 4, 14, 15)
    arrived(relayed, 0)
    late(0)
    stores[0].start()
    arrived(beside, 1)
    early(1)
    arrived(beside, 2)
    early(2)
    arrived(relayed, 1)
    late(1)
    stores[1].start()
    arrived(relayed, 2)
    late(2)
    stores[2].start()

    for copy in v_copies.values():
        copy.wait_send()
    for copies in gathers:
        for copy in copies:
            copy.wait_send()
    for copy in noise_copies.values():
        copy.wait_send()
    for copy in coef_copies.values():
        copy.wait_send()
    for copy in stores:
        copy.wait()


def per_device(noise, v_factors, u_factors, ranks, skew_g, tail_h):
    v, u = v_factors[0], u_factors[0]
    tile, count = noise.shape
    columns = v.shape[1]
    anywhere = pl.BlockSpec(memory_space=pl.ANY)
    dma = pltpu.SemaphoreType.DMA
    gathers = (QUARTERS + HALVES) * 15
    skew, tail = skew_g.reshape(-1, 128), tail_h.reshape(-1, 128)
    return pl.pallas_call(
        kernel,
        out_shape=jax.ShapeDtypeStruct((tile, count), jnp.float32),
        in_specs=[anywhere] * 6,
        out_specs=anywhere,
        scratch_shapes=[
            pltpu.VMEM((tile, count), jnp.bfloat16),
            pltpu.SMEM(ranks.shape, jnp.int32),
            pltpu.VMEM(skew.shape, jnp.float32),
            pltpu.VMEM(tail.shape, jnp.float32),
            pltpu.VMEM((tile, count), jnp.float32),
            pltpu.VMEM((5, count, tile), jnp.bfloat16),
            pltpu.VMEM((tile, columns), jnp.bfloat16),
            pltpu.VMEM((tile, columns), jnp.bfloat16),
            pltpu.VMEM((count, columns // len(SLOTS) * SENT), jnp.bfloat16),
            pltpu.VMEM((count, columns), jnp.bfloat16),
            pltpu.VMEM((tile, 128), jnp.float32),
            pltpu.VMEM((tile, 128), jnp.float32),
            dma((16,)), dma((16,)),
            dma((gathers,)), dma((gathers,)),
            dma((12,)), dma((12,)),
            dma((SENT * 3,)), dma((SENT * 3,)),
            dma((32,)),
        ],
        compiler_params=pltpu.CompilerParams(
            collective_id=0, has_side_effects=True, vmem_limit_bytes=60 * 1024 * 1024
        ),
    )(noise, v, u, ranks, skew, tail)


def solution(mesh):
    placed = (
        P("site", "real"),
        P("site", "real", None),
        P("site", "real", None),
        P(),
        P("site"),
        P("site"),
    )
    return jax.shard_map(
        per_device, mesh=mesh, in_specs=placed, out_specs=P("site", "real"), check_vma=False
    )
```

```python
import functools

import jax
import jax.numpy as jnp
from jax import lax
from jax.experimental import pallas as pl
from jax.experimental.pallas import tpu as pltpu
from jax.sharding import PartitionSpec as P

MESH = pl.DeviceIdType.MESH
CAP = 2
ZS = 8
YS = 4
CHUNKS = ((0, 256), (256, 384), (640, 128))

SLOTS = (
    (0, 1, 0), (1, 1, 0), (-1, 1, 0), (2, 1, 0), (-2, 1, 0),
    (-2, 0, 1), (-2, 1, 1), (2, 0, -1),
    (2, 1, -1), (-2, 0, 2), (2, 1, -2),
    (0, 0, 0), (1, 0, 0), (-1, 0, 0), (2, 0, 0), (-2, 0, 0),
)
SENT = 11
EARLY = ((0, 5), (11, 16))
LATE = (5, 11)
AT = {0: 0, 1: 1, -1: 2, 2: 3, -2: 4}
QUARTERS, HALVES = 4, 2


def tukey(x, g, h):
    y = g * x
    series = y * (1.0 + y * (0.5 + y * (1.0 / 6 + y * (1.0 / 24 + y * (1.0 / 120 + y * (1.0 / 720 + y * (1.0 / 5040)))))))
    lifted = jnp.where(jnp.abs(y) < 0.35, series, jnp.exp(y) - 1.0)
    return lifted / g * jnp.exp(0.5 * h * x * x)


def kernel(noise_hbm, v, u, ranks_hbm, skew_hbm, tail_hbm, out,
           noise, ranks, skew, tail, nt, gv, gu, cs, cr, gb, hb,
           vs, vr, as_, ar, ns, nr, ps, pr, local):
    real, site = lax.axis_index("real"), lax.axis_index("site")
    core = lax.rem(real, 2)
    y = lax.rem(lax.div(real, 2), YS)
    xh = lax.div(real, 2 * YS)
    x = lax.div(site, ZS)
    z = lax.rem(site, ZS)
    rows = v.shape[0]
    unit = v.shape[1] // len(SLOTS)
    rank_block = unit // CAP

    def site_of(fx, dz):
        return (1 - x if fx else x) * ZS + lax.rem(z + dz + ZS, ZS)

    def real_of(fh, dy, fc):
        hi = 1 - xh if fh else xh
        lo = 1 - core if fc else core
        return (hi * YS + lax.rem(y + dy + YS, YS)) * 2 + lo

    def cols(index):
        return pl.ds(pl.multiple_of(index * unit, unit), unit)

    def fixed(index):
        return pl.ds(index * unit, unit)

    def part(c):
        return pl.ds(*CHUNKS[c])

    barrier = pltpu.get_barrier_semaphore()
    peers = [(real, site_of(0, d)) for d in (1, -1, 2, -2)]
    peers += [(real, site_of(1, d)) for d in (0, 1, -1, 2, -2)]
    peers += [(real_of(*w), site) for w in ((1, 0, 0), (0, 1, 0), (0, -1, 0), (0, 0, 1))]
    for peer in peers:
        pl.semaphore_signal(barrier, inc=1, device_id=peer, device_id_type=MESH)

    mine = pl.ds(pl.multiple_of(real * rows, rows), rows)
    loads = []

    def load(source, target):
        loads.append(pltpu.make_async_copy(source, target, local.at[len(loads)]))
        loads[-1].start()

    for c in range(len(CHUNKS)):
        load(noise_hbm.at[:, part(c)], noise.at[:, part(c)])
    load(skew_hbm, skew)
    load(tail_hbm, tail)
    load(ranks_hbm, ranks)
    for m, (dj, fx, di) in enumerate(SLOTS):
        if dj == 0:
            load(v.at[:, cols(site_of(fx, di))], gv.at[mine, fixed(m)])
    for m, (dj, fx, di) in enumerate(SLOTS):
        load(u.at[:, cols(site_of(fx, dj - di))], gu.at[mine, fixed(m)])

    v_copies = {}
    for m, (dj, fx, di) in enumerate(SLOTS):
        if dj != 0:
            v_copies[m] = pltpu.make_async_remote_copy(
                src_ref=v.at[:, cols(site_of(fx, di - dj))], dst_ref=gv.at[mine, fixed(m)],
                send_sem=vs.at[m], recv_sem=vr.at[m],
                device_id=(real, site_of(0, -dj)), device_id_type=MESH,
            )

    KINDS = (
        ((0, 0), (1, 0, 0)),
        ((0, 0), (0, 1, 0)), ((0, 0), (0, -1, 0)),
        ((1, 0), (0, 1, 0)), ((1, 0), (0, -1, 0)),
        ((0, -1), (0, 1, 0)), ((1, 1), (0, -1, 0)),
    ) + tuple((block, (0, 0, 1)) for block in ((0, 0), (1, 0), (0, -1), (0, 1), (1, -1), (1, 1), (0, 2), (1, 2)))
    gathers = []

    def gather(buffer, pieces):
        width = buffer.shape[1] // pieces
        for p in range(pieces):
            copies = []
            for kind, ((fh, dy), to) in enumerate(KINDS):
                owner = real_of(fh, dy, 0)
                block = buffer.at[pl.ds(pl.multiple_of(owner * rows, rows), rows), pl.ds(p * width, width)]
                index = len(gathers) * len(KINDS) + kind
                copies.append(
                    pltpu.make_async_remote_copy(
                        src_ref=block, dst_ref=block, send_sem=as_.at[index], recv_sem=ar.at[index],
                        device_id=(real_of(*to), site), device_id_type=MESH,
                    )
                )
            gathers.append(copies)

    gather(gv, QUARTERS)
    gather(gu, HALVES)
    ua, ub = gathers[QUARTERS], gathers[QUARTERS + 1]

    def start(copies, *kinds):
        for kind in kinds:
            copies[kind].start()

    def step(copies, number):
        if number == 0:
            start(copies, 0, 1, 2, 7)
        elif number == 1:
            copies[0].wait_recv()
            start(copies, 3, 4, 8)
        elif number == 2:
            copies[1].wait_recv()
            start(copies, 5, 9)
            copies[2].wait_recv()
            start(copies, 10)
        elif number == 3:
            copies[4].wait_recv()
            start(copies, 6, 12)
            copies[3].wait_recv()
            start(copies, 11)
        elif number == 4:
            copies[5].wait_recv()
            start(copies, 13)
            copies[6].wait_recv()
            start(copies, 14)
        else:
            for kind in range(7, 15):
                copies[kind].wait_recv()

    def steps(*numbers):
        for quarter, number in numbers:
            step(gathers[quarter], number)

    def noise_copy(c, way, hop):
        return pltpu.make_async_remote_copy(
            src_ref=nt.at[0 if hop == 0 else AT[-way], part(c)],
            dst_ref=nt.at[AT[-way * (hop + 1)], part(c)],
            send_sem=ns.at[(c * 2 + (way > 0)) * 2 + hop], recv_sem=nr.at[(c * 2 + (way > 0)) * 2 + hop],
            device_id=(real, site_of(0, way)), device_id_type=MESH,
        )

    noise_copies = {(c, way, hop): noise_copy(c, way, hop) for c in range(len(CHUNKS)) for way in (1, -1) for hop in (0, 1)}

    def turn(c):
        loads[c].wait()
        nt[0, part(c), :] = noise[:, part(c)].T

    def first(c):
        for way in (1, -1):
            noise_copies[c, way, 0].start()

    def forward(c):
        for way in (1, -1):
            noise_copies[c, way, 0].wait_recv()
            noise_copies[c, way, 1].start()

    def far(c):
        for way in (1, -1):
            noise_copies[c, way, 1].wait_recv()

    def coef_copy(m, c):
        dj, fx, di = SLOTS[m]
        return pltpu.make_async_remote_copy(
            src_ref=cs.at[part(c), fixed(m)], dst_ref=cr.at[part(c), fixed(m)],
            send_sem=ps.at[m * len(CHUNKS) + c], recv_sem=pr.at[m * len(CHUNKS) + c],
            device_id=(real, site_of(fx, di)), device_id_type=MESH,
        )

    coef_copies = {(m, c): coef_copy(m, c) for m in range(SENT) for c in range(len(CHUNKS))}
    level = lax.broadcasted_iota(jnp.int32, (1, unit), 1) // rank_block

    def project(m, c):
        dj, fx, di = SLOTS[m]
        projected = jnp.dot(nt[AT[dj], part(c), :], gv[:, fixed(m)], preferred_element_type=jnp.float32)
        alive = (level < ranks[site_of(fx, di), site_of(0, dj)]).astype(jnp.float32)
        (cs if m < SENT else cr)[part(c), fixed(m)] = (projected * alive).astype(jnp.bfloat16)

    def projects(c, *slots):
        waiting = None
        for m in slots:
            project(m, c)
            if waiting is not None:
                coef_copies[waiting, c].start()
            waiting = m if m < SENT else None
        if waiting is not None:
            coef_copies[waiting, c].start()

    def dot_t(left, right):
        return lax.dot_general(left, right, (((1,), (1,)), ((), ())), preferred_element_type=jnp.float32)

    block = 256

    def early(c):
        @pl.loop(0, out.shape[0] // block)
        def _(k):
            here = pl.ds(pl.multiple_of(k * block, block), block)
            total = None
            for lo, hi in EARLY:
                span = pl.ds(lo * unit, (hi - lo) * unit)
                term = dot_t(gu[here, span], cr[part(c), span])
                total = term if total is None else total + term
            out[here, part(c)] = total

    def late(c):
        begin, width = CHUNKS[c]

        @pl.loop(0, out.shape[0] // block)
        def _(k):
            here = pl.ds(pl.multiple_of(k * block, block), block)
            span = pl.ds(LATE[0] * unit, (LATE[1] - LATE[0]) * unit)
            total = out[here, part(c)] + dot_t(gu[here, span], cr[part(c), span])
            g, h = gb[here, :], hb[here, :]
            for q in range(0, width, 128):
                out[here, pl.ds(begin + q, 128)] = tukey(total[:, q:q + 128], g, h)

    def arrived(slots, c):
        for m in slots:
            coef_copies[m, c].wait_recv()

    beside = range(5)
    relayed = range(5, SENT)
    turn(0)
    pl.semaphore_wait(barrier, len(peers))
    for m in v_copies:
        v_copies[m].start()
    turn(1)
    first(0)
    turn(2)
    first(1)
    for copy in loads[len(CHUNKS):]:
        copy.wait()
    start(ua, 0, 7)
    for k in range(skew.shape[0]):
        spread = pl.ds(k * 128, 128)
        gb[spread, :] = jnp.broadcast_to(skew[pl.ds(k, 1), :], (128, 128)).T
        hb[spread, :] = jnp.broadcast_to(tail[pl.ds(k, 1), :], (128, 128)).T

    def ready(quarter):
        count = len(SLOTS) // QUARTERS
        for m in range(quarter * count, (quarter + 1) * count):
            if m in v_copies:
                v_copies[m].wait_recv()
        step(gathers[quarter], 0)

    ready(0)
    steps((0, 1))
    ready(1)
    steps((0, 2), (1, 1))
    ready(2)
    steps((0, 3), (1, 2), (2, 1))
    ready(3)
    start(ub, 0, 7)
    steps((0, 4), (1, 3), (2, 2), (3, 1))
    forward(0)
    first(2)
    steps((0, 5))
    projects(0, 0)
    projects(1, 0)
    steps((1, 4), (2, 3), (3, 2))
    start(ua, 1, 2)
    projects(0, 1, 2)
    steps((1, 5), (2, 4), (3, 3))
    step(ua, 1)
    projects(2, 0)
    forward(1)
    projects(1, 1, 2)
    steps((2, 5), (3, 4))
    step(ua, 2)
    start(ub, 1, 2)
    steps((3, 5))
    far(0)
    projects(0, 9, 10, 5, 6, 7, 8, 3, 4)
    step(ua, 3)
    step(ub, 1)
    forward(2)
    projects(2, 1, 2)
    projects(0, 11, 12, 13, 14, 15)
    step(ua, 4)
    step(ub, 2)
    projects(1, 11, 12, 13)
    projects(2, 11, 12, 13)
    step(ub, 3)
    far(1)
    projects(1, 9, 10, 5, 6, 7, 8, 3, 4)
    step(ub, 4)
    projects(1, 14, 15)
    step(ua, 5)
    step(ub, 5)
    arrived(beside, 0)
    early(0)
    far(2)
    projects(2, 9, 10, 5, 6, 7, 8, 3, 4, 14, 15)
    arrived(relayed, 0)
    late(0)
    arrived(beside, 1)
    early(1)
    arrived(beside, 2)
    early(2)
    arrived(relayed, 1)
    late(1)
    arrived(relayed, 2)
    late(2)

    for copy in v_copies.values():
        copy.wait_send()
    for copies in gathers:
        for copy in copies:
            copy.wait_send()
    for copy in noise_copies.values():
        copy.wait_send()
    for copy in coef_copies.values():
        copy.wait_send()


def per_device(noise, v_factors, u_factors, ranks, skew_g, tail_h):
    v, u = v_factors[0], u_factors[0]
    tile, count = noise.shape
    columns = v.shape[1]
    anywhere = pl.BlockSpec(memory_space=pl.ANY)
    dma = pltpu.SemaphoreType.DMA
    gathers = (QUARTERS + HALVES) * 15
    skew, tail = skew_g.reshape(-1, 128), tail_h.reshape(-1, 128)
    return pl.pallas_call(
        kernel,
        out_shape=pltpu.VMEM((tile, count), jnp.float32),
        in_specs=[anywhere] * 6,
        out_specs=pl.BlockSpec(memory_space=pltpu.VMEM),
        scratch_shapes=[
            pltpu.VMEM((tile, count), jnp.bfloat16),
            pltpu.SMEM(ranks.shape, jnp.int32),
            pltpu.VMEM(skew.shape, jnp.float32),
            pltpu.VMEM(tail.shape, jnp.float32),
            pltpu.VMEM((5, count, tile), jnp.bfloat16),
            pltpu.VMEM((tile, columns), jnp.bfloat16),
            pltpu.VMEM((tile, columns), jnp.bfloat16),
            pltpu.VMEM((count, columns // len(SLOTS) * SENT), jnp.bfloat16),
            pltpu.VMEM((count, columns), jnp.bfloat16),
            pltpu.VMEM((tile, 128), jnp.float32),
            pltpu.VMEM((tile, 128), jnp.float32),
            dma((16,)), dma((16,)),
            dma((gathers,)), dma((gathers,)),
            dma((12,)), dma((12,)),
            dma((SENT * 3,)), dma((SENT * 3,)),
            dma((32,)),
        ],
        compiler_params=pltpu.CompilerParams(
            collective_id=0, has_side_effects=True, vmem_limit_bytes=60 * 1024 * 1024
        ),
    )(noise, v, u, ranks, skew, tail)


def solution(mesh):
    placed = (
        P("site", "real"),
        P("site", "real", None),
        P("site", "real", None),
        P(),
        P("site"),
        P("site"),
    )
    return jax.shard_map(
        per_device, mesh=mesh, in_specs=placed, out_specs=P("site", "real"), check_vma=False
    )
```

```python
import functools

import jax
import jax.numpy as jnp
from jax import lax
from jax.experimental import pallas as pl
from jax.experimental.pallas import tpu as pltpu
from jax.sharding import PartitionSpec as P

MESH = pl.DeviceIdType.MESH
CAP = 2
ZS = 8
YS = 4
CHUNKS = ((0, 256), (256, 384), (640, 128))

SLOTS = (
    (0, 1, 0), (1, 1, 0), (-1, 1, 0), (2, 1, 0), (-2, 1, 0),
    (-2, 0, 1), (-2, 1, 1), (2, 0, -1),
    (2, 1, -1), (-2, 0, 2), (2, 1, -2),
    (0, 0, 0), (1, 0, 0), (-1, 0, 0), (2, 0, 0), (-2, 0, 0),
)
SENT = 11
EARLY = ((0, 5), (11, 16))
LATE = (5, 11)
AT = {0: 0, 1: 1, -1: 2, 2: 3, -2: 4}
QUARTERS, HALVES = 4, 2


def tukey(x, g, h):
    y = g * x
    series = y * (1.0 + y * (0.5 + y * (1.0 / 6 + y * (1.0 / 24 + y * (1.0 / 120 + y * (1.0 / 720 + y * (1.0 / 5040)))))))
    lifted = jnp.where(jnp.abs(y) < 0.35, series, jnp.exp(y) - 1.0)
    return lifted / g * jnp.exp(0.5 * h * x * x)


def kernel(noise_hbm, v, u, ranks_hbm, skew_hbm, tail_hbm, out,
           noise, ranks, skew, tail, nt, gv, gu, cs, cr, gb, hb,
           sent, vr, ar, nr, pr, local):
    real, site = lax.axis_index("real"), lax.axis_index("site")
    core = lax.rem(real, 2)
    y = lax.rem(lax.div(real, 2), YS)
    xh = lax.div(real, 2 * YS)
    x = lax.div(site, ZS)
    z = lax.rem(site, ZS)
    rows = v.shape[0]
    unit = v.shape[1] // len(SLOTS)
    rank_block = unit // CAP

    def site_of(fx, dz):
        return (1 - x if fx else x) * ZS + lax.rem(z + dz + ZS, ZS)

    def real_of(fh, dy, fc):
        hi = 1 - xh if fh else xh
        lo = 1 - core if fc else core
        return (hi * YS + lax.rem(y + dy + YS, YS)) * 2 + lo

    def cols(index):
        return pl.ds(pl.multiple_of(index * unit, unit), unit)

    def fixed(index):
        return pl.ds(index * unit, unit)

    def part(c):
        return pl.ds(*CHUNKS[c])

    barrier = pltpu.get_barrier_semaphore()
    peers = [(real, site_of(0, d)) for d in (1, -1, 2, -2)]
    peers += [(real, site_of(1, d)) for d in (0, 1, -1, 2, -2)]
    peers += [(real_of(*w), site) for w in ((1, 0, 0), (0, 1, 0), (0, -1, 0), (0, 0, 1))]
    for peer in peers:
        pl.semaphore_signal(barrier, inc=1, device_id=peer, device_id_type=MESH)

    mine = pl.ds(pl.multiple_of(real * rows, rows), rows)
    resident = [m for m in range(len(SLOTS)) if SLOTS[m][0] == 0]

    def load(source, target, index):
        copy = pltpu.make_async_copy(source, target, local.at[index])
        copy.start()
        return copy

    def take(semaphore, like):
        pltpu.make_async_copy(like, like, semaphore).wait()

    noise_loads = [load(noise_hbm.at[:, part(c)], noise.at[:, part(c)], c) for c in range(len(CHUNKS))]
    small_loads = [load(skew_hbm, skew, 3), load(tail_hbm, tail, 4), load(ranks_hbm, ranks, 5)]
    for m in resident:
        dj, fx, di = SLOTS[m]
        load(v.at[:, cols(site_of(fx, di))], gv.at[mine, fixed(m)], 6)
    for m, (dj, fx, di) in enumerate(SLOTS):
        load(u.at[:, cols(site_of(fx, dj - di))], gu.at[mine, fixed(m)], 7)

    v_copies = {}
    for m, (dj, fx, di) in enumerate(SLOTS):
        if dj != 0:
            v_copies[m] = pltpu.make_async_remote_copy(
                src_ref=v.at[:, cols(site_of(fx, di - dj))], dst_ref=gv.at[mine, fixed(m)],
                send_sem=sent.at[0], recv_sem=vr.at[m * QUARTERS // len(SLOTS)],
                device_id=(real, site_of(0, -dj)), device_id_type=MESH,
            )

    KINDS = (
        ((0, 0), (1, 0, 0)),
        ((0, 0), (0, 1, 0)), ((0, 0), (0, -1, 0)),
        ((1, 0), (0, 1, 0)), ((1, 0), (0, -1, 0)),
        ((0, -1), (0, 1, 0)), ((1, 1), (0, -1, 0)),
    ) + tuple((block, (0, 0, 1)) for block in ((0, 0), (1, 0), (0, -1), (0, 1), (1, -1), (1, 1), (0, 2), (1, 2)))
    GROUPS = (0, 1, 1, 2, 2, 3, 3) + (4,) * 8
    gathers = []
    gathered = []

    def gather(buffer, pieces, sender):
        width = buffer.shape[1] // pieces
        for p in range(pieces):
            copies = []
            for kind, ((fh, dy), to) in enumerate(KINDS):
                owner = real_of(fh, dy, 0)
                block = buffer.at[pl.ds(pl.multiple_of(owner * rows, rows), rows), pl.ds(p * width, width)]
                index = len(gathers) * 5 + GROUPS[kind]
                copies.append(
                    pltpu.make_async_remote_copy(
                        src_ref=block, dst_ref=block, send_sem=sent.at[sender], recv_sem=ar.at[index],
                        device_id=(real_of(*to), site), device_id_type=MESH,
                    )
                )
            gathers.append(copies)
            gathered.append((buffer, width))

    gather(gv, QUARTERS, 1)
    gather(gu, HALVES, 2)
    ua, ub = QUARTERS, QUARTERS + 1

    def start(piece, *kinds):
        for kind in kinds:
            gathers[piece][kind].start()

    def step(piece, number):
        buffer, width = gathered[piece]
        if number > 0:
            blocks = (1, 2, 2, 2, 8)[number - 1]
            take(ar.at[piece * 5 + number - 1], buffer.at[pl.ds(0, blocks * rows), pl.ds(0, width)])
        start(piece, *((0, 1, 2, 7), (3, 4, 8), (5, 9, 10), (6, 12, 11), (13, 14), ())[number])

    def steps(*numbers):
        for quarter, number in numbers:
            step(quarter, number)

    def noise_copy(c, way, hop):
        return pltpu.make_async_remote_copy(
            src_ref=nt.at[0 if hop == 0 else AT[-way], part(c)],
            dst_ref=nt.at[AT[-way * (hop + 1)], part(c)],
            send_sem=sent.at[3], recv_sem=nr.at[c * 2 + hop],
            device_id=(real, site_of(0, way)), device_id_type=MESH,
        )

    noise_copies = {(c, way, hop): noise_copy(c, way, hop) for c in range(len(CHUNKS)) for way in (1, -1) for hop in (0, 1)}

    def turn(c):
        noise_loads[c].wait()
        nt[0, part(c), :] = noise[:, part(c)].T

    def first(c):
        for way in (1, -1):
            noise_copies[c, way, 0].start()

    def forward(c):
        take(nr.at[c * 2], nt.at[pl.ds(1, 2), part(c)])
        for way in (1, -1):
            noise_copies[c, way, 1].start()

    def far(c):
        take(nr.at[c * 2 + 1], nt.at[pl.ds(3, 2), part(c)])

    def coef_copy(m, c):
        dj, fx, di = SLOTS[m]
        return pltpu.make_async_remote_copy(
            src_ref=cs.at[part(c), fixed(m)], dst_ref=cr.at[part(c), fixed(m)],
            send_sem=sent.at[4], recv_sem=pr.at[c * 2 + (m >= LATE[0])],
            device_id=(real, site_of(fx, di)), device_id_type=MESH,
        )

    coef_copies = {(m, c): coef_copy(m, c) for m in range(SENT) for c in range(len(CHUNKS))}
    level = lax.broadcasted_iota(jnp.int32, (1, unit), 1) // rank_block

    def project(m, c):
        dj, fx, di = SLOTS[m]
        projected = jnp.dot(nt[AT[dj], part(c), :], gv[:, fixed(m)], preferred_element_type=jnp.float32)
        alive = (level < ranks[site_of(fx, di), site_of(0, dj)]).astype(jnp.float32)
        (cs if m < SENT else cr)[part(c), fixed(m)] = (projected * alive).astype(jnp.bfloat16)

    def projects(c, *slots):
        waiting = None
        for m in slots:
            project(m, c)
            if waiting is not None:
                coef_copies[waiting, c].start()
            waiting = m if m < SENT else None
        if waiting is not None:
            coef_copies[waiting, c].start()

    def dot_t(left, right):
        return lax.dot_general(left, right, (((1,), (1,)), ((), ())), preferred_element_type=jnp.float32)

    block = 512

    def early(c):
        @pl.loop(0, out.shape[0] // block)
        def _(k):
            here = pl.ds(pl.multiple_of(k * block, block), block)
            total = None
            for lo, hi in EARLY:
                span = pl.ds(lo * unit, (hi - lo) * unit)
                term = dot_t(gu[here, span], cr[part(c), span])
                total = term if total is None else total + term
            out[here, part(c)] = total

    def late(c):
        begin, width = CHUNKS[c]

        @pl.loop(0, out.shape[0] // block)
        def _(k):
            here = pl.ds(pl.multiple_of(k * block, block), block)
            span = pl.ds(LATE[0] * unit, (LATE[1] - LATE[0]) * unit)
            total = out[here, part(c)] + dot_t(gu[here, span], cr[part(c), span])
            g, h = gb[here, :], hb[here, :]
            for q in range(0, width, 128):
                out[here, pl.ds(begin + q, 128)] = tukey(total[:, q:q + 128], g, h)

    def arrived(late_slots, c):
        slots = LATE[1] - LATE[0] if late_slots else LATE[0]
        take(pr.at[c * 2 + late_slots], cr.at[part(c), pl.ds(0, slots * unit)])

    beside, relayed = 0, 1
    pl.semaphore_wait(barrier, len(peers))
    for m in v_copies:
        v_copies[m].start()
    turn(0)
    turn(1)
    first(0)
    turn(2)
    first(1)
    take(local.at[6], gv.at[pl.ds(0, rows), pl.ds(0, len(resident) * unit)])
    take(local.at[7], gu.at[pl.ds(0, rows), :])
    for copy in small_loads:
        copy.wait()
    for k in range(skew.shape[0]):
        spread = pl.ds(k * 128, 128)
        gb[spread, :] = jnp.broadcast_to(skew[pl.ds(k, 1), :], (128, 128)).T
        hb[spread, :] = jnp.broadcast_to(tail[pl.ds(k, 1), :], (128, 128)).T

    def ready(quarter):
        count = len(SLOTS) // QUARTERS
        coming = sum(m in v_copies for m in range(quarter * count, (quarter + 1) * count))
        take(vr.at[quarter], gv.at[pl.ds(0, rows), pl.ds(0, coming * unit)])
        step(quarter, 0)

    ready(0)
    steps((0, 1), (0, 2))
    ready(1)
    start(ua, 0, 7)
    steps((0, 3), (1, 1))
    ready(2)
    steps((0, 4), (1, 2), (0, 5))
    projects(0, 0)
    projects(1, 0)
    projects(2, 0)
    ready(3)
    steps((1, 3), (2, 1))
    forward(0)
    first(2)
    projects(0, 1, 2)
    steps((1, 4), (2, 2), (3, 1))
    steps((1, 5), (2, 3), (3, 2))
    start(ua, 1, 2)
    steps((2, 4), (3, 3), (2, 5))
    forward(1)
    projects(1, 1, 2)
    step(ua, 1)
    start(ub, 0, 7)
    steps((3, 4), (3, 5))
    step(ua, 2)
    start(ub, 1, 2)
    far(0)
    projects(0, 3, 4)
    forward(2)
    projects(0, 9, 10, 5, 6, 7, 8)
    step(ua, 3)
    step(ub, 1)
    projects(2, 1, 2)
    projects(0, 11, 12, 13, 14, 15)
    projects(1, 11, 12, 13)
    projects(2, 11, 12, 13)
    step(ua, 4)
    step(ub, 2)
    far(1)
    projects(1, 3, 4, 9, 10, 5, 6, 7, 8)
    far(2)
    projects(2, 3, 4, 9, 10, 5, 6, 7, 8)
    step(ub, 3)
    step(ub, 4)
    step(ua, 5)
    step(ub, 5)
    projects(1, 14, 15)
    projects(2, 14, 15)
    arrived(beside, 0)
    early(0)
    arrived(relayed, 0)
    late(0)
    arrived(beside, 1)
    early(1)
    arrived(beside, 2)
    early(2)
    arrived(relayed, 1)
    late(1)
    arrived(relayed, 2)
    late(2)

    take(sent.at[0], gv.at[pl.ds(0, rows), pl.ds(0, len(v_copies) * unit)])
    take(sent.at[1], gv.at[pl.ds(0, 15 * rows), :])
    take(sent.at[2], gu.at[pl.ds(0, 15 * rows), :])
    take(sent.at[3], nt.at[pl.ds(0, 4)])
    take(sent.at[4], cs)


def per_device(noise, v_factors, u_factors, ranks, skew_g, tail_h):
    v, u = v_factors[0], u_factors[0]
    tile, count = noise.shape
    columns = v.shape[1]
    anywhere = pl.BlockSpec(memory_space=pl.ANY)
    dma = pltpu.SemaphoreType.DMA
    skew, tail = skew_g.reshape(-1, 128), tail_h.reshape(-1, 128)
    return pl.pallas_call(
        kernel,
        out_shape=pltpu.VMEM((tile, count), jnp.float32),
        in_specs=[anywhere] * 6,
        out_specs=pl.BlockSpec(memory_space=pltpu.VMEM),
        scratch_shapes=[
            pltpu.VMEM((tile, count), jnp.bfloat16),
            pltpu.SMEM(ranks.shape, jnp.int32),
            pltpu.VMEM(skew.shape, jnp.float32),
            pltpu.VMEM(tail.shape, jnp.float32),
            pltpu.VMEM((5, count, tile), jnp.bfloat16),
            pltpu.VMEM((tile, columns), jnp.bfloat16),
            pltpu.VMEM((tile, columns), jnp.bfloat16),
            pltpu.VMEM((count, columns // len(SLOTS) * SENT), jnp.bfloat16),
            pltpu.VMEM((count, columns), jnp.bfloat16),
            pltpu.VMEM((tile, 128), jnp.float32),
            pltpu.VMEM((tile, 128), jnp.float32),
            dma((5,)),
            dma((QUARTERS,)),
            dma(((QUARTERS + HALVES) * 5,)),
            dma((2 * len(CHUNKS),)),
            dma((2 * len(CHUNKS),)),
            dma((8,)),
        ],
        compiler_params=pltpu.CompilerParams(
            collective_id=0, has_side_effects=True, vmem_limit_bytes=60 * 1024 * 1024
        ),
    )(noise, v, u, ranks, skew, tail)


def solution(mesh):
    placed = (
        P("site", "real"),
        P("site", "real", None),
        P("site", "real", None),
        P(),
        P("site"),
        P("site"),
    )
    return jax.shard_map(
        per_device, mesh=mesh, in_specs=placed, out_specs=P("site", "real"), check_vma=False
    )
```

```python
import functools

import jax
import jax.numpy as jnp
from jax import lax
from jax.experimental import pallas as pl
from jax.experimental.pallas import tpu as pltpu
from jax.sharding import PartitionSpec as P

MESH = pl.DeviceIdType.MESH
CAP = 2
ZS = 8
YS = 4
CHUNKS = ((0, 256), (256, 256), (512, 256))

SLOTS = (
    (0, 1, 0), (1, 1, 0), (-1, 1, 0), (2, 1, 0), (-2, 1, 0),
    (-2, 0, 1), (-2, 1, 1), (2, 0, -1),
    (2, 1, -1), (-2, 0, 2), (2, 1, -2),
    (0, 0, 0), (1, 0, 0), (-1, 0, 0), (2, 0, 0), (-2, 0, 0),
)
SENT = 11
EARLY = ((0, 5), (11, 16))
LATE = (5, 9, 11)
AT = {0: 0, 1: 1, -1: 2, 2: 3, -2: 4}
QUARTERS, HALVES = 4, 2


def tukey(x, g, h):
    y = g * x
    series = y * (1.0 + y * (0.5 + y * (1.0 / 6 + y * (1.0 / 24 + y * (1.0 / 120 + y * (1.0 / 720 + y * (1.0 / 5040)))))))
    lifted = jnp.where(jnp.abs(y) < 0.35, series, jnp.exp(y) - 1.0)
    return lifted / g * jnp.exp(0.5 * h * x * x)


def kernel(noise_hbm, v, u, ranks_hbm, skew_hbm, tail_hbm, out,
           noise, ranks, skew, tail, nt, gv, gu, cs, cr, gb, hb,
           sent, vr, ar, nr, pr, local):
    real, site = lax.axis_index("real"), lax.axis_index("site")
    core = lax.rem(real, 2)
    y = lax.rem(lax.div(real, 2), YS)
    xh = lax.div(real, 2 * YS)
    x = lax.div(site, ZS)
    z = lax.rem(site, ZS)
    rows = v.shape[0]
    unit = v.shape[1] // len(SLOTS)
    rank_block = unit // CAP

    def site_of(fx, dz):
        return (1 - x if fx else x) * ZS + lax.rem(z + dz + ZS, ZS)

    def real_of(fh, dy, fc):
        hi = 1 - xh if fh else xh
        lo = 1 - core if fc else core
        return (hi * YS + lax.rem(y + dy + YS, YS)) * 2 + lo

    def cols(index):
        return pl.ds(pl.multiple_of(index * unit, unit), unit)

    def fixed(index):
        return pl.ds(index * unit, unit)

    def part(c):
        return pl.ds(*CHUNKS[c])

    barrier = pltpu.get_barrier_semaphore()
    peers = [(real, site_of(1, d)) for d in (2, -2, 1, -1)]
    peers += [(real, site_of(0, d)) for d in (2, -2, 1, -1)]
    peers += [(real, site_of(1, 0))]
    peers += [(real_of(*w), site) for w in ((1, 0, 0), (0, 1, 0), (0, -1, 0), (0, 0, 1))]
    for peer in peers:
        pl.semaphore_signal(barrier, inc=1, device_id=peer, device_id_type=MESH)

    mine = pl.ds(pl.multiple_of(real * rows, rows), rows)
    resident = [m for m in range(len(SLOTS)) if SLOTS[m][0] == 0]

    def load(source, target, index):
        copy = pltpu.make_async_copy(source, target, local.at[index])
        copy.start()
        return copy

    def take(semaphore, like):
        pltpu.make_async_copy(like, like, semaphore).wait()

    noise_loads = [load(noise_hbm.at[:, part(c)], noise.at[:, part(c)], c) for c in range(len(CHUNKS))]
    small_loads = [load(skew_hbm, skew, 3), load(tail_hbm, tail, 4), load(ranks_hbm, ranks, 5)]
    for m in resident:
        dj, fx, di = SLOTS[m]
        load(v.at[:, cols(site_of(fx, di))], gv.at[mine, fixed(m)], 6)
    for m, (dj, fx, di) in enumerate(SLOTS):
        load(u.at[:, cols(site_of(fx, dj - di))], gu.at[mine, fixed(m)], 7)

    v_copies = {}
    for m, (dj, fx, di) in enumerate(SLOTS):
        if dj != 0:
            v_copies[m] = pltpu.make_async_remote_copy(
                src_ref=v.at[:, cols(site_of(fx, di - dj))], dst_ref=gv.at[mine, fixed(m)],
                send_sem=sent.at[0], recv_sem=vr.at[m * QUARTERS // len(SLOTS)],
                device_id=(real, site_of(0, -dj)), device_id_type=MESH,
            )

    KINDS = (
        ((0, 0), (1, 0, 0)),
        ((0, 0), (0, 1, 0)), ((0, 0), (0, -1, 0)),
        ((1, 0), (0, 1, 0)), ((1, 0), (0, -1, 0)),
        ((0, -1), (0, 1, 0)), ((1, 1), (0, -1, 0)),
    ) + tuple((block, (0, 0, 1)) for block in ((0, 0), (1, 0), (0, -1), (0, 1), (1, -1), (1, 1), (0, 2), (1, 2)))
    GROUPS = (0, 1, 1, 2, 2, 3, 3) + (4,) * 8
    gathers = []
    gathered = []

    def gather(buffer, pieces, sender):
        width = buffer.shape[1] // pieces
        for p in range(pieces):
            copies = []
            for kind, ((fh, dy), to) in enumerate(KINDS):
                owner = real_of(fh, dy, 0)
                block = buffer.at[pl.ds(pl.multiple_of(owner * rows, rows), rows), pl.ds(p * width, width)]
                index = len(gathers) * 5 + GROUPS[kind]
                copies.append(
                    pltpu.make_async_remote_copy(
                        src_ref=block, dst_ref=block, send_sem=sent.at[sender], recv_sem=ar.at[index],
                        device_id=(real_of(*to), site), device_id_type=MESH,
                    )
                )
            gathers.append(copies)
            gathered.append((buffer, width))

    gather(gv, QUARTERS, 1)
    gather(gu, HALVES, 2)
    ua, ub = QUARTERS, QUARTERS + 1

    def start(piece, *kinds):
        for kind in kinds:
            gathers[piece][kind].start()

    def step(piece, number):
        buffer, width = gathered[piece]
        if number > 0:
            blocks = (1, 2, 2, 2, 8)[number - 1]
            take(ar.at[piece * 5 + number - 1], buffer.at[pl.ds(0, blocks * rows), pl.ds(0, width)])
        start(piece, *((0, 1, 2, 7), (3, 4, 8), (5, 9, 10), (6, 12, 11), (13, 14), ())[number])

    def steps(*numbers):
        for quarter, number in numbers:
            step(quarter, number)

    def noise_copy(c, way, hop):
        return pltpu.make_async_remote_copy(
            src_ref=nt.at[0 if hop == 0 else AT[-way], part(c)],
            dst_ref=nt.at[AT[-way * (hop + 1)], part(c)],
            send_sem=sent.at[3], recv_sem=nr.at[c * 2 + hop],
            device_id=(real, site_of(0, way)), device_id_type=MESH,
        )

    noise_copies = {(c, way, hop): noise_copy(c, way, hop) for c in range(len(CHUNKS)) for way in (1, -1) for hop in (0, 1)}

    def turn(c):
        noise_loads[c].wait()
        nt[0, part(c), :] = noise[:, part(c)].T

    def first(c):
        for way in (1, -1):
            noise_copies[c, way, 0].start()

    def forward(c):
        take(nr.at[c * 2], nt.at[pl.ds(1, 2), part(c)])
        for way in (1, -1):
            noise_copies[c, way, 1].start()

    def far(c):
        take(nr.at[c * 2 + 1], nt.at[pl.ds(3, 2), part(c)])

    def coef_copy(m, c):
        dj, fx, di = SLOTS[m]
        return pltpu.make_async_remote_copy(
            src_ref=cs.at[part(c), fixed(m)], dst_ref=cr.at[part(c), fixed(m)],
            send_sem=sent.at[4], recv_sem=pr.at[c * 3 + (m >= LATE[0]) + (m >= LATE[1])],
            device_id=(real, site_of(fx, di)), device_id_type=MESH,
        )

    coef_copies = {(m, c): coef_copy(m, c) for m in range(SENT) for c in range(len(CHUNKS))}
    level = lax.broadcasted_iota(jnp.int32, (1, unit), 1) // rank_block

    def project(m, c):
        dj, fx, di = SLOTS[m]
        projected = jnp.dot(nt[AT[dj], part(c), :], gv[:, fixed(m)], preferred_element_type=jnp.float32)
        alive = (level < ranks[site_of(fx, di), site_of(0, dj)]).astype(jnp.float32)
        (cs if m < SENT else cr)[part(c), fixed(m)] = (projected * alive).astype(jnp.bfloat16)

    def projects(c, *slots):
        waiting = None
        for m in slots:
            project(m, c)
            if waiting is not None:
                coef_copies[waiting, c].start()
            waiting = m if m < SENT else None
        if waiting is not None:
            coef_copies[waiting, c].start()

    def dot_t(left, right):
        return lax.dot_general(left, right, (((1,), (1,)), ((), ())), preferred_element_type=jnp.float32)

    block = 512

    def product(here, c, lo, hi):
        span = pl.ds(lo * unit, (hi - lo) * unit)
        return dot_t(gu[here, span], cr[part(c), span])

    def blocks():
        return pl.loop(0, out.shape[0] // block)

    def rows_of(k):
        return pl.ds(pl.multiple_of(k * block, block), block)

    def early(c):
        @blocks()
        def _(k):
            out[rows_of(k), part(c)] = product(rows_of(k), c, *EARLY[0]) + product(rows_of(k), c, *EARLY[1])

    def middle(c):
        @blocks()
        def _(k):
            out[rows_of(k), part(c)] += product(rows_of(k), c, LATE[1], LATE[2])

    def late(c, first_slot, last_slot=LATE[2]):
        begin, width = CHUNKS[c]

        @blocks()
        def _(k):
            here = rows_of(k)
            total = out[here, part(c)] + product(here, c, first_slot, last_slot)
            g, h = gb[here, :], hb[here, :]
            for q in range(0, width, 128):
                out[here, pl.ds(begin + q, 128)] = tukey(total[:, q:q + 128], g, h)

    def arrived(group, c):
        slots = (LATE[0], LATE[1] - LATE[0], LATE[2] - LATE[1])[group]
        take(pr.at[c * 3 + group], cr.at[part(c), pl.ds(0, slots * unit)])

    beside, near, distant = 0, 1, 2
    pl.semaphore_wait(barrier, len(peers))
    for m in v_copies:
        v_copies[m].start()
    turn(0)
    turn(1)
    first(0)
    turn(2)
    first(1)
    take(local.at[6], gv.at[pl.ds(0, rows), pl.ds(0, len(resident) * unit)])
    take(local.at[7], gu.at[pl.ds(0, rows), :])
    for copy in small_loads:
        copy.wait()
    for k in range(skew.shape[0]):
        spread = pl.ds(k * 128, 128)
        gb[spread, :] = jnp.broadcast_to(skew[pl.ds(k, 1), :], (128, 128)).T
        hb[spread, :] = jnp.broadcast_to(tail[pl.ds(k, 1), :], (128, 128)).T

    def ready(quarter):
        count = len(SLOTS) // QUARTERS
        coming = sum(m in v_copies for m in range(quarter * count, (quarter + 1) * count))
        take(vr.at[quarter], gv.at[pl.ds(0, rows), pl.ds(0, coming * unit)])
        step(quarter, 0)

    ready(0)
    steps((0, 1), (0, 2))
    start(ua, 0, 7)
    steps((0, 3))
    ready(1)
    ready(2)
    steps((0, 4), (0, 5))
    projects(0, 0)
    projects(1, 0)
    projects(2, 0)
    ready(3)
    steps((1, 1), (1, 2))
    forward(0)
    first(2)
    projects(0, 1, 2)
    steps((2, 1), (1, 3), (2, 2), (3, 1))
    steps((1, 4), (2, 3), (3, 2))
    forward(1)
    projects(1, 1, 2)
    start(ub, 0, 7)
    start(ua, 1, 2)
    steps((1, 5), (2, 4), (3, 3))
    steps((2, 5), (3, 4), (3, 5))
    step(ua, 1)
    start(ub, 1, 2)
    far(0)
    projects(0, 3, 4)
    step(ua, 2)
    forward(2)
    projects(0, 9, 10, 5, 6, 7, 8)
    projects(2, 1, 2)
    step(ua, 3)
    step(ub, 1)
    projects(0, 11, 12, 13, 14, 15)
    projects(1, 11, 12, 13)
    projects(2, 11, 12, 13)
    step(ua, 4)
    step(ub, 2)
    far(1)
    projects(1, 3, 4, 9, 10, 5, 6, 7, 8)
    far(2)
    projects(2, 3, 4, 9, 10, 5, 6, 7, 8)
    step(ub, 3)
    step(ub, 4)
    step(ua, 5)
    step(ub, 5)
    projects(1, 14, 15)
    projects(2, 14, 15)
    arrived(beside, 0)
    early(0)
    arrived(near, 0)
    arrived(distant, 0)
    late(0, LATE[0])
    arrived(beside, 1)
    early(1)
    arrived(beside, 2)
    early(2)
    arrived(near, 1)
    arrived(distant, 1)
    late(1, LATE[0])
    arrived(distant, 2)
    middle(2)
    arrived(near, 2)
    late(2, LATE[0], LATE[1])

    take(sent.at[0], gv.at[pl.ds(0, rows), pl.ds(0, len(v_copies) * unit)])
    take(sent.at[1], gv.at[pl.ds(0, 15 * rows), :])
    take(sent.at[2], gu.at[pl.ds(0, 15 * rows), :])
    take(sent.at[3], nt.at[pl.ds(0, 4)])
    take(sent.at[4], cs)


def per_device(noise, v_factors, u_factors, ranks, skew_g, tail_h):
    v, u = v_factors[0], u_factors[0]
    tile, count = noise.shape
    columns = v.shape[1]
    anywhere = pl.BlockSpec(memory_space=pl.ANY)
    dma = pltpu.SemaphoreType.DMA
    skew, tail = skew_g.reshape(-1, 128), tail_h.reshape(-1, 128)
    return pl.pallas_call(
        kernel,
        out_shape=pltpu.VMEM((tile, count), jnp.float32),
        in_specs=[anywhere] * 6,
        out_specs=pl.BlockSpec(memory_space=pltpu.VMEM),
        scratch_shapes=[
            pltpu.VMEM((tile, count), jnp.bfloat16),
            pltpu.SMEM(ranks.shape, jnp.int32),
            pltpu.VMEM(skew.shape, jnp.float32),
            pltpu.VMEM(tail.shape, jnp.float32),
            pltpu.VMEM((5, count, tile), jnp.bfloat16),
            pltpu.VMEM((tile, columns), jnp.bfloat16),
            pltpu.VMEM((tile, columns), jnp.bfloat16),
            pltpu.VMEM((count, columns // len(SLOTS) * SENT), jnp.bfloat16),
            pltpu.VMEM((count, columns), jnp.bfloat16),
            pltpu.VMEM((tile, 128), jnp.float32),
            pltpu.VMEM((tile, 128), jnp.float32),
            dma((5,)),
            dma((QUARTERS,)),
            dma(((QUARTERS + HALVES) * 5,)),
            dma((2 * len(CHUNKS),)),
            dma((3 * len(CHUNKS),)),
            dma((8,)),
        ],
        compiler_params=pltpu.CompilerParams(
            collective_id=0, has_side_effects=True, vmem_limit_bytes=60 * 1024 * 1024
        ),
    )(noise, v, u, ranks, skew, tail)


def solution(mesh):
    placed = (
        P("site", "real"),
        P("site", "real", None),
        P("site", "real", None),
        P(),
        P("site"),
        P("site"),
    )
    return jax.shard_map(
        per_device, mesh=mesh, in_specs=placed, out_specs=P("site", "real"), check_vma=False
    )
```

```python
import functools

import jax
import jax.numpy as jnp
from jax import lax
from jax.experimental import pallas as pl
from jax.experimental.pallas import tpu as pltpu
from jax.sharding import PartitionSpec as P

MESH = pl.DeviceIdType.MESH
CAP = 2
ZS = 8
YS = 4
CHUNKS = ((0, 256), (256, 256), (512, 256))

SLOTS = (
    (0, 1, 0), (1, 1, 0), (-1, 1, 0), (2, 1, 0), (-2, 1, 0),
    (-2, 0, 1), (2, 0, -1), (-2, 1, 1),
    (2, 1, -1), (-2, 0, 2), (2, 1, -2),
    (0, 0, 0), (1, 0, 0), (-1, 0, 0), (2, 0, 0), (-2, 0, 0),
)
SENT = 11
EARLY = ((0, 5), (11, 16))
LATE = (5, 7, 9, 11)
AT = {0: 0, 1: 1, -1: 2, 2: 3, -2: 4}
QUARTERS, HALVES = 4, 2


def tukey(x, g, h):
    y = g * x
    series = y * (1.0 + y * (0.5 + y * (1.0 / 6 + y * (1.0 / 24 + y * (1.0 / 120 + y * (1.0 / 720 + y * (1.0 / 5040)))))))
    lifted = jnp.where(jnp.abs(y) < 0.35, series, jnp.exp(y) - 1.0)
    return lifted / g * jnp.exp(0.5 * h * x * x)


def kernel(noise_hbm, v, u, ranks_hbm, skew_hbm, tail_hbm, out,
           noise, ranks, skew, tail, nt, gv, gu, cs, cr, gb, hb,
           sent, vr, ar, nr, pr, local):
    real, site = lax.axis_index("real"), lax.axis_index("site")
    core = lax.rem(real, 2)
    y = lax.rem(lax.div(real, 2), YS)
    xh = lax.div(real, 2 * YS)
    x = lax.div(site, ZS)
    z = lax.rem(site, ZS)
    rows = v.shape[0]
    unit = v.shape[1] // len(SLOTS)
    rank_block = unit // CAP

    def site_of(fx, dz):
        return (1 - x if fx else x) * ZS + lax.rem(z + dz + ZS, ZS)

    def real_of(fh, dy, fc):
        hi = 1 - xh if fh else xh
        lo = 1 - core if fc else core
        return (hi * YS + lax.rem(y + dy + YS, YS)) * 2 + lo

    def cols(index):
        return pl.ds(pl.multiple_of(index * unit, unit), unit)

    def fixed(index):
        return pl.ds(index * unit, unit)

    def part(c):
        return pl.ds(*CHUNKS[c])

    barrier = pltpu.get_barrier_semaphore()
    peers = [(real, site_of(1, d)) for d in (2, -2, 1, -1)]
    peers += [(real, site_of(0, d)) for d in (2, -2, 1, -1)]
    peers += [(real, site_of(1, 0))]
    peers += [(real_of(*w), site) for w in ((1, 0, 0), (0, 1, 0), (0, -1, 0), (0, 0, 1))]
    for peer in peers:
        pl.semaphore_signal(barrier, inc=1, device_id=peer, device_id_type=MESH)

    mine = pl.ds(pl.multiple_of(real * rows, rows), rows)
    resident = [m for m in range(len(SLOTS)) if SLOTS[m][0] == 0]

    def load(source, target, index):
        copy = pltpu.make_async_copy(source, target, local.at[index])
        copy.start()
        return copy

    def take(semaphore, like):
        pltpu.make_async_copy(like, like, semaphore).wait()

    noise_loads = [load(noise_hbm.at[:, part(c)], noise.at[:, part(c)], c) for c in range(len(CHUNKS))]
    small_loads = [load(skew_hbm, skew, 3), load(tail_hbm, tail, 4), load(ranks_hbm, ranks, 5)]
    for m in resident:
        dj, fx, di = SLOTS[m]
        load(v.at[:, cols(site_of(fx, di))], gv.at[mine, fixed(m)], 6)
    for m, (dj, fx, di) in enumerate(SLOTS):
        load(u.at[:, cols(site_of(fx, dj - di))], gu.at[mine, fixed(m)], 7)

    v_copies = {}
    for m, (dj, fx, di) in enumerate(SLOTS):
        if dj != 0:
            v_copies[m] = pltpu.make_async_remote_copy(
                src_ref=v.at[:, cols(site_of(fx, di - dj))], dst_ref=gv.at[mine, fixed(m)],
                send_sem=sent.at[0], recv_sem=vr.at[m * QUARTERS // len(SLOTS)],
                device_id=(real, site_of(0, -dj)), device_id_type=MESH,
            )

    KINDS = (
        ((0, 0), (1, 0, 0)),
        ((0, 0), (0, 1, 0)), ((0, 0), (0, -1, 0)),
        ((1, 0), (0, 1, 0)), ((1, 0), (0, -1, 0)),
        ((0, -1), (0, 1, 0)), ((1, 1), (0, -1, 0)),
    ) + tuple((block, (0, 0, 1)) for block in ((0, 0), (1, 0), (0, -1), (0, 1), (1, -1), (1, 1), (0, 2), (1, 2)))
    GROUPS = (0, 1, 1, 2, 2, 3, 3) + (4,) * 8
    gathers = []
    gathered = []

    def gather(buffer, pieces, sender):
        width = buffer.shape[1] // pieces
        for p in range(pieces):
            copies = []
            for kind, ((fh, dy), to) in enumerate(KINDS):
                owner = real_of(fh, dy, 0)
                block = buffer.at[pl.ds(pl.multiple_of(owner * rows, rows), rows), pl.ds(p * width, width)]
                index = len(gathers) * 5 + GROUPS[kind]
                copies.append(
                    pltpu.make_async_remote_copy(
                        src_ref=block, dst_ref=block, send_sem=sent.at[sender], recv_sem=ar.at[index],
                        device_id=(real_of(*to), site), device_id_type=MESH,
                    )
                )
            gathers.append(copies)
            gathered.append((buffer, width))

    gather(gv, QUARTERS, 1)
    gather(gu, HALVES, 2)
    ua, ub = QUARTERS, QUARTERS + 1

    def start(piece, *kinds):
        for kind in kinds:
            gathers[piece][kind].start()

    def step(piece, number):
        buffer, width = gathered[piece]
        if number > 0:
            blocks = (1, 2, 2, 2, 8)[number - 1]
            take(ar.at[piece * 5 + number - 1], buffer.at[pl.ds(0, blocks * rows), pl.ds(0, width)])
        start(piece, *((0, 1, 2, 7), (3, 4, 8), (5, 9, 10), (6, 12, 11), (13, 14), ())[number])

    def steps(*numbers):
        for quarter, number in numbers:
            step(quarter, number)

    def noise_copy(c, way, hop):
        return pltpu.make_async_remote_copy(
            src_ref=nt.at[0 if hop == 0 else AT[-way], part(c)],
            dst_ref=nt.at[AT[-way * (hop + 1)], part(c)],
            send_sem=sent.at[3], recv_sem=nr.at[c * 2 + hop],
            device_id=(real, site_of(0, way)), device_id_type=MESH,
        )

    noise_copies = {(c, way, hop): noise_copy(c, way, hop) for c in range(len(CHUNKS)) for way in (1, -1) for hop in (0, 1)}

    def turn(c):
        noise_loads[c].wait()
        nt[0, part(c), :] = noise[:, part(c)].T

    def first(c):
        for way in (1, -1):
            noise_copies[c, way, 0].start()

    def forward(c):
        take(nr.at[c * 2], nt.at[pl.ds(1, 2), part(c)])
        for way in (1, -1):
            noise_copies[c, way, 1].start()

    def far(c):
        take(nr.at[c * 2 + 1], nt.at[pl.ds(3, 2), part(c)])

    def coef_copy(m, c):
        dj, fx, di = SLOTS[m]
        return pltpu.make_async_remote_copy(
            src_ref=cs.at[part(c), fixed(m)], dst_ref=cr.at[part(c), fixed(m)],
            send_sem=sent.at[4], recv_sem=pr.at[c * 4 + sum(m >= first for first in LATE[:3])],
            device_id=(real, site_of(fx, di)), device_id_type=MESH,
        )

    coef_copies = {(m, c): coef_copy(m, c) for m in range(SENT) for c in range(len(CHUNKS))}
    level = lax.broadcasted_iota(jnp.int32, (1, unit), 1) // rank_block

    def project(m, c):
        dj, fx, di = SLOTS[m]
        projected = jnp.dot(nt[AT[dj], part(c), :], gv[:, fixed(m)], preferred_element_type=jnp.float32)
        alive = (level < ranks[site_of(fx, di), site_of(0, dj)]).astype(jnp.float32)
        (cs if m < SENT else cr)[part(c), fixed(m)] = (projected * alive).astype(jnp.bfloat16)

    def projects(c, *slots):
        waiting = None
        for m in slots:
            project(m, c)
            if waiting is not None:
                coef_copies[waiting, c].start()
            waiting = m if m < SENT else None
        if waiting is not None:
            coef_copies[waiting, c].start()

    def dot_t(left, right):
        return lax.dot_general(left, right, (((1,), (1,)), ((), ())), preferred_element_type=jnp.float32)

    block = 512

    def product(here, c, lo, hi):
        span = pl.ds(lo * unit, (hi - lo) * unit)
        return dot_t(gu[here, span], cr[part(c), span])

    def blocks():
        return pl.loop(0, out.shape[0] // block)

    def rows_of(k):
        return pl.ds(pl.multiple_of(k * block, block), block)

    def early(c):
        @blocks()
        def _(k):
            out[rows_of(k), part(c)] = product(rows_of(k), c, *EARLY[0]) + product(rows_of(k), c, *EARLY[1])

    def middle(c, group):
        @blocks()
        def _(k):
            out[rows_of(k), part(c)] += product(rows_of(k), c, LATE[group], LATE[group + 1])

    def late(c, start_slot, end):
        begin, width = CHUNKS[c]

        @blocks()
        def _(k):
            here = rows_of(k)
            total = out[here, part(c)] + product(here, c, start_slot, end)
            g, h = gb[here, :], hb[here, :]
            for q in range(0, width, 128):
                out[here, pl.ds(begin + q, 128)] = tukey(total[:, q:q + 128], g, h)

    def arrived(c, *groups):
        for group in groups:
            slots = LATE[0] if group < 0 else LATE[group + 1] - LATE[group]
            take(pr.at[c * 4 + group + 1], cr.at[part(c), pl.ds(0, slots * unit)])

    pl.semaphore_wait(barrier, len(peers))
    for m in v_copies:
        v_copies[m].start()
    turn(0)
    turn(1)
    first(0)
    turn(2)
    first(1)
    take(local.at[6], gv.at[pl.ds(0, rows), pl.ds(0, len(resident) * unit)])
    take(local.at[7], gu.at[pl.ds(0, rows), :])
    for copy in small_loads:
        copy.wait()
    for k in range(skew.shape[0]):
        spread = pl.ds(k * 128, 128)
        gb[spread, :] = jnp.broadcast_to(skew[pl.ds(k, 1), :], (128, 128)).T
        hb[spread, :] = jnp.broadcast_to(tail[pl.ds(k, 1), :], (128, 128)).T

    def ready(quarter):
        count = len(SLOTS) // QUARTERS
        coming = sum(m in v_copies for m in range(quarter * count, (quarter + 1) * count))
        take(vr.at[quarter], gv.at[pl.ds(0, rows), pl.ds(0, coming * unit)])
        step(quarter, 0)

    ready(0)
    steps((0, 1), (0, 2))
    start(ua, 0, 7)
    steps((0, 3))
    ready(1)
    ready(2)
    steps((0, 4), (0, 5))
    projects(0, 0)
    projects(1, 0)
    projects(2, 0)
    ready(3)
    steps((1, 1), (1, 2))
    forward(0)
    projects(0, 1, 2)
    steps((2, 1), (1, 3), (2, 2), (3, 1))
    steps((1, 4), (2, 3), (3, 2))
    forward(1)
    first(2)
    projects(1, 1, 2)
    start(ub, 0, 7)
    start(ua, 1, 2)
    steps((1, 5), (2, 4), (3, 3))
    far(0)
    projects(0, 3, 4)
    steps((2, 5), (3, 4), (3, 5))
    step(ua, 1)
    start(ub, 1, 2)
    projects(0, 9, 10, 7, 8)
    far(1)
    projects(1, 3, 4)
    step(ua, 2)
    projects(0, 11, 12, 13, 14, 15)
    projects(1, 11, 12, 13, 14, 15)
    step(ua, 3)
    step(ub, 1)
    forward(2)
    projects(0, 5, 6)
    projects(1, 9, 10, 5, 6, 7, 8)
    projects(2, 1, 2)
    projects(2, 11, 12, 13)
    step(ua, 4)
    step(ub, 2)
    far(2)
    projects(2, 3, 4, 9, 10, 5, 6, 7, 8)
    step(ub, 3)
    step(ub, 4)
    step(ua, 5)
    step(ub, 5)
    projects(2, 14, 15)
    arrived(0, -1)
    early(0)
    arrived(0, 0, 1, 2)
    late(0, LATE[0], LATE[3])
    arrived(1, -1)
    early(1)
    arrived(2, -1)
    early(2)
    arrived(1, 0, 1, 2)
    late(1, LATE[0], LATE[3])
    arrived(2, 2)
    middle(2, 2)
    arrived(2, 0)
    middle(2, 0)
    arrived(2, 1)
    late(2, LATE[1], LATE[2])

    take(sent.at[0], gv.at[pl.ds(0, rows), pl.ds(0, len(v_copies) * unit)])
    take(sent.at[1], gv.at[pl.ds(0, 15 * rows), :])
    take(sent.at[2], gu.at[pl.ds(0, 15 * rows), :])
    take(sent.at[3], nt.at[pl.ds(0, 4)])
    take(sent.at[4], cs)


def per_device(noise, v_factors, u_factors, ranks, skew_g, tail_h):
    v, u = v_factors[0], u_factors[0]
    tile, count = noise.shape
    columns = v.shape[1]
    anywhere = pl.BlockSpec(memory_space=pl.ANY)
    dma = pltpu.SemaphoreType.DMA
    skew, tail = skew_g.reshape(-1, 128), tail_h.reshape(-1, 128)
    return pl.pallas_call(
        kernel,
        out_shape=pltpu.VMEM((tile, count), jnp.float32),
        in_specs=[anywhere] * 6,
        out_specs=pl.BlockSpec(memory_space=pltpu.VMEM),
        scratch_shapes=[
            pltpu.VMEM((tile, count), jnp.bfloat16),
            pltpu.SMEM(ranks.shape, jnp.int32),
            pltpu.VMEM(skew.shape, jnp.float32),
            pltpu.VMEM(tail.shape, jnp.float32),
            pltpu.VMEM((5, count, tile), jnp.bfloat16),
            pltpu.VMEM((tile, columns), jnp.bfloat16),
            pltpu.VMEM((tile, columns), jnp.bfloat16),
            pltpu.VMEM((count, columns // len(SLOTS) * SENT), jnp.bfloat16),
            pltpu.VMEM((count, columns), jnp.bfloat16),
            pltpu.VMEM((tile, 128), jnp.float32),
            pltpu.VMEM((tile, 128), jnp.float32),
            dma((5,)),
            dma((QUARTERS,)),
            dma(((QUARTERS + HALVES) * 5,)),
            dma((2 * len(CHUNKS),)),
            dma((4 * len(CHUNKS),)),
            dma((8,)),
        ],
        compiler_params=pltpu.CompilerParams(
            collective_id=0, has_side_effects=True, vmem_limit_bytes=60 * 1024 * 1024
        ),
    )(noise, v, u, ranks, skew, tail)


def solution(mesh):
    placed = (
        P("site", "real"),
        P("site", "real", None),
        P("site", "real", None),
        P(),
        P("site"),
        P("site"),
    )
    return jax.shard_map(
        per_device, mesh=mesh, in_specs=placed, out_specs=P("site", "real"), check_vma=False
    )
```

```python
import functools

import jax
import jax.numpy as jnp
from jax import lax
from jax.experimental import pallas as pl
from jax.experimental.pallas import tpu as pltpu
from jax.sharding import PartitionSpec as P

MESH = pl.DeviceIdType.MESH
CAP = 2
ZS = 8
YS = 4
CHUNKS = ((0, 256), (256, 256), (512, 256))

SLOTS = (
    (0, 1, 0), (1, 1, 0), (-1, 1, 0), (2, 1, 0), (-2, 1, 0),
    (-2, 0, 1), (2, 0, -1), (-2, 1, 1),
    (2, 1, -1), (-2, 0, 2), (2, 1, -2),
    (0, 0, 0), (1, 0, 0), (-1, 0, 0), (2, 0, 0), (-2, 0, 0),
)
SENT = 11
EARLY = ((0, 5), (11, 16))
LATE = (5, 7, 9, 11)
AT = {0: 0, 1: 1, -1: 2, 2: 3, -2: 4}
QUARTERS, HALVES = 4, 2


def tukey(x, g, h):
    y = g * x
    series = y * (1.0 + y * (0.5 + y * (1.0 / 6 + y * (1.0 / 24 + y * (1.0 / 120 + y * (1.0 / 720 + y * (1.0 / 5040)))))))
    lifted = jnp.where(jnp.abs(y) < 0.35, series, jnp.exp(y) - 1.0)
    return lifted / g * jnp.exp(0.5 * h * x * x)


def kernel(noise_hbm, v, u, ranks_hbm, skew_hbm, tail_hbm, out,
           noise, ranks, skew, tail, nt, gv, gu, cs, cr, gb, hb,
           sent, vr, ar, nr, pr, local):
    real, site = lax.axis_index("real"), lax.axis_index("site")
    core = lax.rem(real, 2)
    y = lax.rem(lax.div(real, 2), YS)
    xh = lax.div(real, 2 * YS)
    x = lax.div(site, ZS)
    z = lax.rem(site, ZS)
    rows = v.shape[0]
    unit = v.shape[1] // len(SLOTS)
    rank_block = unit // CAP

    def site_of(fx, dz):
        return (1 - x if fx else x) * ZS + lax.rem(z + dz + ZS, ZS)

    def real_of(fh, dy, fc):
        hi = 1 - xh if fh else xh
        lo = 1 - core if fc else core
        return (hi * YS + lax.rem(y + dy + YS, YS)) * 2 + lo

    def cols(index):
        return pl.ds(pl.multiple_of(index * unit, unit), unit)

    def fixed(index):
        return pl.ds(index * unit, unit)

    def part(c):
        return pl.ds(*CHUNKS[c])

    barrier = pltpu.get_barrier_semaphore()
    peers = [(real, site_of(1, d)) for d in (2, -2, 1, -1)]
    peers += [(real, site_of(0, d)) for d in (2, -2, 1, -1)]
    peers += [(real, site_of(1, 0))]
    peers += [(real_of(*w), site) for w in ((1, 0, 0), (0, 1, 0), (0, -1, 0), (0, 0, 1))]
    for peer in peers:
        pl.semaphore_signal(barrier, inc=1, device_id=peer, device_id_type=MESH)

    mine = pl.ds(pl.multiple_of(real * rows, rows), rows)
    resident = [m for m in range(len(SLOTS)) if SLOTS[m][0] == 0]

    def load(source, target, index):
        copy = pltpu.make_async_copy(source, target, local.at[index])
        copy.start()
        return copy

    def take(semaphore, like):
        pltpu.make_async_copy(like, like, semaphore).wait()

    noise_loads = [load(noise_hbm.at[:, part(c)], noise.at[:, part(c)], c) for c in range(len(CHUNKS))]
    small_loads = [load(skew_hbm, skew, 3), load(tail_hbm, tail, 4), load(ranks_hbm, ranks, 5)]
    for m in resident:
        dj, fx, di = SLOTS[m]
        load(v.at[:, cols(site_of(fx, di))], gv.at[mine, fixed(m)], 6)
    for m, (dj, fx, di) in enumerate(SLOTS):
        load(u.at[:, cols(site_of(fx, dj - di))], gu.at[mine, fixed(m)], 7)

    v_copies = {}
    for m, (dj, fx, di) in enumerate(SLOTS):
        if dj != 0:
            v_copies[m] = pltpu.make_async_remote_copy(
                src_ref=v.at[:, cols(site_of(fx, di - dj))], dst_ref=gv.at[mine, fixed(m)],
                send_sem=sent.at[0], recv_sem=vr.at[m * QUARTERS // len(SLOTS)],
                device_id=(real, site_of(0, -dj)), device_id_type=MESH,
            )

    KINDS = (
        ((0, 0), (1, 0, 0)),
        ((0, 0), (0, 1, 0)), ((0, 0), (0, -1, 0)),
        ((1, 0), (0, 1, 0)), ((1, 0), (0, -1, 0)),
        ((0, -1), (0, 1, 0)), ((1, 1), (0, -1, 0)),
    ) + tuple((block, (0, 0, 1)) for block in ((0, 0), (1, 0), (0, -1), (0, 1), (1, -1), (1, 1), (0, 2), (1, 2)))
    GROUPS = (0, 1, 1, 2, 2, 3, 3) + (4,) * 8
    gathers = []
    gathered = []

    def gather(buffer, pieces, sender):
        width = buffer.shape[1] // pieces
        for p in range(pieces):
            copies = []
            for kind, ((fh, dy), to) in enumerate(KINDS):
                owner = real_of(fh, dy, 0)
                block = buffer.at[pl.ds(pl.multiple_of(owner * rows, rows), rows), pl.ds(p * width, width)]
                index = len(gathers) * 5 + GROUPS[kind]
                copies.append(
                    pltpu.make_async_remote_copy(
                        src_ref=block, dst_ref=block, send_sem=sent.at[sender], recv_sem=ar.at[index],
                        device_id=(real_of(*to), site), device_id_type=MESH,
                    )
                )
            gathers.append(copies)
            gathered.append((buffer, width))

    gather(gv, QUARTERS, 1)
    gather(gu, HALVES, 2)
    ua, ub = QUARTERS, QUARTERS + 1

    def start(piece, *kinds):
        for kind in kinds:
            gathers[piece][kind].start()

    def step(piece, number):
        buffer, width = gathered[piece]
        if number > 0:
            blocks = (1, 2, 2, 2, 8)[number - 1]
            take(ar.at[piece * 5 + number - 1], buffer.at[pl.ds(0, blocks * rows), pl.ds(0, width)])
        start(piece, *((0, 1, 2, 7), (3, 4, 8), (5, 9, 10), (6, 12, 11), (13, 14), ())[number])

    def steps(*numbers):
        for quarter, number in numbers:
            step(quarter, number)

    def noise_copy(c, way, hop):
        return pltpu.make_async_remote_copy(
            src_ref=nt.at[0 if hop == 0 else AT[-way], part(c)],
            dst_ref=nt.at[AT[-way * (hop + 1)], part(c)],
            send_sem=sent.at[3], recv_sem=nr.at[c * 2 + hop],
            device_id=(real, site_of(0, way)), device_id_type=MESH,
        )

    noise_copies = {(c, way, hop): noise_copy(c, way, hop) for c in range(len(CHUNKS)) for way in (1, -1) for hop in (0, 1)}

    def turn(c):
        noise_loads[c].wait()
        nt[0, part(c), :] = noise[:, part(c)].T

    def first(c):
        for way in (1, -1):
            noise_copies[c, way, 0].start()

    def forward(c):
        take(nr.at[c * 2], nt.at[pl.ds(1, 2), part(c)])
        for way in (1, -1):
            noise_copies[c, way, 1].start()

    def far(c):
        take(nr.at[c * 2 + 1], nt.at[pl.ds(3, 2), part(c)])

    def coef_copy(m, c):
        dj, fx, di = SLOTS[m]
        return pltpu.make_async_remote_copy(
            src_ref=cs.at[part(c), fixed(m)], dst_ref=cr.at[part(c), fixed(m)],
            send_sem=sent.at[4], recv_sem=pr.at[c * 4 + sum(m >= first for first in LATE[:3])],
            device_id=(real, site_of(fx, di)), device_id_type=MESH,
        )

    coef_copies = {(m, c): coef_copy(m, c) for m in range(SENT) for c in range(len(CHUNKS))}
    level = lax.broadcasted_iota(jnp.int32, (1, unit), 1) // rank_block

    def project(m, c):
        dj, fx, di = SLOTS[m]
        projected = jnp.dot(nt[AT[dj], part(c), :], gv[:, fixed(m)], preferred_element_type=jnp.float32)
        alive = (level < ranks[site_of(fx, di), site_of(0, dj)]).astype(jnp.float32)
        (cs if m < SENT else cr)[part(c), fixed(m)] = (projected * alive).astype(jnp.bfloat16)

    def projects(c, *slots):
        waiting = None
        for m in slots:
            project(m, c)
            if waiting is not None:
                coef_copies[waiting, c].start()
            waiting = m if m < SENT else None
        if waiting is not None:
            coef_copies[waiting, c].start()

    def dot_t(left, right):
        return lax.dot_general(left, right, (((1,), (1,)), ((), ())), preferred_element_type=jnp.float32)

    block = 512

    def product(here, c, lo, hi):
        span = pl.ds(lo * unit, (hi - lo) * unit)
        return dot_t(gu[here, span], cr[part(c), span])

    def blocks():
        return pl.loop(0, out.shape[0] // block)

    def rows_of(k):
        return pl.ds(pl.multiple_of(k * block, block), block)

    def early(c):
        @blocks()
        def _(k):
            out[rows_of(k), part(c)] = product(rows_of(k), c, *EARLY[0]) + product(rows_of(k), c, *EARLY[1])

    def middle(c, group):
        @blocks()
        def _(k):
            out[rows_of(k), part(c)] += product(rows_of(k), c, LATE[group], LATE[group + 1])

    def late(c, start_slot, end):
        begin, width = CHUNKS[c]

        @blocks()
        def _(k):
            here = rows_of(k)
            total = out[here, part(c)] + product(here, c, start_slot, end)
            g, h = gb[here, :], hb[here, :]
            for q in range(0, width, 128):
                out[here, pl.ds(begin + q, 128)] = tukey(total[:, q:q + 128], g, h)

    def arrived(c, *groups):
        for group in groups:
            slots = LATE[0] if group < 0 else LATE[group + 1] - LATE[group]
            take(pr.at[c * 4 + group + 1], cr.at[part(c), pl.ds(0, slots * unit)])

    pl.semaphore_wait(barrier, len(peers))
    for m in v_copies:
        v_copies[m].start()
    turn(0)
    turn(1)
    first(0)
    turn(2)
    first(1)
    take(local.at[6], gv.at[pl.ds(0, rows), pl.ds(0, len(resident) * unit)])
    take(local.at[7], gu.at[pl.ds(0, rows), :])
    for copy in small_loads:
        copy.wait()
    for k in range(skew.shape[0]):
        spread = pl.ds(k * 128, 128)
        gb[spread, :] = jnp.broadcast_to(skew[pl.ds(k, 1), :], (128, 128)).T
        hb[spread, :] = jnp.broadcast_to(tail[pl.ds(k, 1), :], (128, 128)).T

    def ready(quarter):
        count = len(SLOTS) // QUARTERS
        coming = sum(m in v_copies for m in range(quarter * count, (quarter + 1) * count))
        take(vr.at[quarter], gv.at[pl.ds(0, rows), pl.ds(0, coming * unit)])
        step(quarter, 0)

    ready(0)
    steps((0, 1), (0, 2))
    start(ua, 0, 7)
    steps((0, 3))
    ready(1)
    ready(2)
    steps((0, 4), (0, 5))
    projects(0, 0)
    projects(1, 0)
    projects(2, 0)
    ready(3)
    steps((1, 1), (1, 2))
    forward(0)
    projects(0, 1, 2)
    steps((2, 1), (1, 3), (2, 2), (3, 1))
    steps((1, 4), (2, 3), (3, 2))
    forward(1)
    first(2)
    projects(1, 1, 2)
    start(ub, 0, 7)
    start(ua, 1, 2)
    steps((1, 5), (2, 4), (3, 3))
    far(0)
    projects(0, 3, 4)
    steps((2, 5), (3, 4), (3, 5))
    step(ua, 1)
    start(ub, 1, 2)
    projects(0, 9, 10, 7, 8)
    far(1)
    projects(1, 3, 4)
    step(ua, 2)
    projects(0, 11, 12, 13, 14, 15)
    projects(1, 11, 12, 13, 14, 15)
    step(ua, 3)
    step(ub, 1)
    forward(2)
    projects(0, 5, 6)
    projects(1, 9, 10, 7, 8, 5, 6)
    projects(2, 1, 2)
    projects(2, 11, 12, 13)
    step(ua, 4)
    step(ub, 2)
    far(2)
    projects(2, 3, 4, 9, 10, 5, 6, 7, 8)
    step(ub, 3)
    step(ub, 4)
    step(ua, 5)
    step(ub, 5)
    projects(2, 14, 15)
    arrived(0, -1)
    early(0)
    arrived(0, 0, 1, 2)
    late(0, LATE[0], LATE[3])
    arrived(1, -1)
    early(1)
    arrived(2, -1)
    early(2)
    arrived(1, 0, 1, 2)
    late(1, LATE[0], LATE[3])
    arrived(2, 2)
    middle(2, 2)
    arrived(2, 0)
    middle(2, 0)
    arrived(2, 1)
    late(2, LATE[1], LATE[2])

    take(sent.at[0], gv.at[pl.ds(0, rows), pl.ds(0, len(v_copies) * unit)])
    take(sent.at[1], gv.at[pl.ds(0, 15 * rows), :])
    take(sent.at[2], gu.at[pl.ds(0, 15 * rows), :])
    take(sent.at[3], nt.at[pl.ds(0, 4)])
    take(sent.at[4], cs)


def per_device(noise, v_factors, u_factors, ranks, skew_g, tail_h):
    v, u = v_factors[0], u_factors[0]
    tile, count = noise.shape
    columns = v.shape[1]
    anywhere = pl.BlockSpec(memory_space=pl.ANY)
    dma = pltpu.SemaphoreType.DMA
    skew, tail = skew_g.reshape(-1, 128), tail_h.reshape(-1, 128)
    return pl.pallas_call(
        kernel,
        out_shape=pltpu.VMEM((tile, count), jnp.float32),
        in_specs=[anywhere] * 6,
        out_specs=pl.BlockSpec(memory_space=pltpu.VMEM),
        scratch_shapes=[
            pltpu.VMEM((tile, count), jnp.bfloat16),
            pltpu.SMEM(ranks.shape, jnp.int32),
            pltpu.VMEM(skew.shape, jnp.float32),
            pltpu.VMEM(tail.shape, jnp.float32),
            pltpu.VMEM((5, count, tile), jnp.bfloat16),
            pltpu.VMEM((tile, columns), jnp.bfloat16),
            pltpu.VMEM((tile, columns), jnp.bfloat16),
            pltpu.VMEM((count, columns // len(SLOTS) * SENT), jnp.bfloat16),
            pltpu.VMEM((count, columns), jnp.bfloat16),
            pltpu.VMEM((tile, 128), jnp.float32),
            pltpu.VMEM((tile, 128), jnp.float32),
            dma((5,)),
            dma((QUARTERS,)),
            dma(((QUARTERS + HALVES) * 5,)),
            dma((2 * len(CHUNKS),)),
            dma((4 * len(CHUNKS),)),
            dma((8,)),
        ],
        compiler_params=pltpu.CompilerParams(
            collective_id=0, has_side_effects=True, vmem_limit_bytes=60 * 1024 * 1024
        ),
    )(noise, v, u, ranks, skew, tail)


def solution(mesh):
    placed = (
        P("site", "real"),
        P("site", "real", None),
        P("site", "real", None),
        P(),
        P("site"),
        P("site"),
    )
    return jax.shard_map(
        per_device, mesh=mesh, in_specs=placed, out_specs=P("site", "real"), check_vma=False
    )
```

```python
import functools

import jax
import jax.numpy as jnp
from jax import lax
from jax.experimental import pallas as pl
from jax.experimental.pallas import tpu as pltpu
from jax.sharding import PartitionSpec as P

MESH = pl.DeviceIdType.MESH
CAP = 2
ZS = 8
YS = 4
CHUNKS = ((0, 256), (256, 256), (512, 256))

SLOTS = (
    (0, 1, 0), (1, 1, 0), (-1, 1, 0), (2, 1, 0), (-2, 1, 0),
    (-2, 0, 1), (2, 0, -1), (-2, 1, 1),
    (2, 1, -1), (-2, 0, 2), (2, 1, -2),
    (0, 0, 0), (1, 0, 0), (-1, 0, 0), (2, 0, 0), (-2, 0, 0),
)
SENT = 11
EARLY = ((0, 5), (11, 16))
LATE = (5, 7, 9, 11)
AT = {0: 0, 1: 1, -1: 2, 2: 3, -2: 4}
QUARTERS, HALVES = 4, 2


def tukey(x, g, inverse_g, half_h):
    y = g * x
    series = y * (1.0 + y * (0.5 + y * (1.0 / 6 + y * (1.0 / 24 + y * (1.0 / 120 + y * (1.0 / 720 + y * (1.0 / 5040)))))))
    lifted = jnp.where(jnp.abs(y) < 0.35, series, jnp.exp(y) - 1.0)
    return lifted * inverse_g * jnp.exp(half_h * x * x)


def kernel(noise_hbm, v, u, ranks_hbm, skew_hbm, tail_hbm, out,
           noise, ranks, skew, tail, nt, gv, gu, cs, cr, gb, ib, hb,
           sent, vr, ar, nr, pr, local):
    real, site = lax.axis_index("real"), lax.axis_index("site")
    core = lax.rem(real, 2)
    y = lax.rem(lax.div(real, 2), YS)
    xh = lax.div(real, 2 * YS)
    x = lax.div(site, ZS)
    z = lax.rem(site, ZS)
    rows = v.shape[0]
    unit = v.shape[1] // len(SLOTS)
    rank_block = unit // CAP

    def site_of(fx, dz):
        return (1 - x if fx else x) * ZS + lax.rem(z + dz + ZS, ZS)

    def real_of(fh, dy, fc):
        hi = 1 - xh if fh else xh
        lo = 1 - core if fc else core
        return (hi * YS + lax.rem(y + dy + YS, YS)) * 2 + lo

    def cols(index):
        return pl.ds(pl.multiple_of(index * unit, unit), unit)

    def fixed(index):
        return pl.ds(index * unit, unit)

    def part(c):
        return pl.ds(*CHUNKS[c])

    barrier = pltpu.get_barrier_semaphore()
    peers = [(real, site_of(1, d)) for d in (2, -2, 1, -1)]
    peers += [(real, site_of(0, d)) for d in (2, -2, 1, -1)]
    peers += [(real, site_of(1, 0))]
    peers += [(real_of(*w), site) for w in ((1, 0, 0), (0, 1, 0), (0, -1, 0), (0, 0, 1))]
    for peer in peers:
        pl.semaphore_signal(barrier, inc=1, device_id=peer, device_id_type=MESH)

    mine = pl.ds(pl.multiple_of(real * rows, rows), rows)
    resident = [m for m in range(len(SLOTS)) if SLOTS[m][0] == 0]

    def load(source, target, index):
        copy = pltpu.make_async_copy(source, target, local.at[index])
        copy.start()
        return copy

    def take(semaphore, like):
        pltpu.make_async_copy(like, like, semaphore).wait()

    noise_loads = [load(noise_hbm.at[:, part(c)], noise.at[:, part(c)], c) for c in range(len(CHUNKS))]
    small_loads = [load(skew_hbm, skew, 3), load(tail_hbm, tail, 4), load(ranks_hbm, ranks, 5)]
    for m in resident:
        dj, fx, di = SLOTS[m]
        load(v.at[:, cols(site_of(fx, di))], gv.at[mine, fixed(m)], 6)
    for m, (dj, fx, di) in enumerate(SLOTS):
        load(u.at[:, cols(site_of(fx, dj - di))], gu.at[mine, fixed(m)], 7)

    v_copies = {}
    for m, (dj, fx, di) in enumerate(SLOTS):
        if dj != 0:
            v_copies[m] = pltpu.make_async_remote_copy(
                src_ref=v.at[:, cols(site_of(fx, di - dj))], dst_ref=gv.at[mine, fixed(m)],
                send_sem=sent.at[0], recv_sem=vr.at[m * QUARTERS // len(SLOTS)],
                device_id=(real, site_of(0, -dj)), device_id_type=MESH,
            )

    KINDS = (
        ((0, 0), (1, 0, 0)),
        ((0, 0), (0, 1, 0)), ((0, 0), (0, -1, 0)),
        ((1, 0), (0, 1, 0)), ((1, 0), (0, -1, 0)),
        ((0, -1), (0, 1, 0)), ((1, 1), (0, -1, 0)),
    ) + tuple((block, (0, 0, 1)) for block in ((0, 0), (1, 0), (0, -1), (0, 1), (1, -1), (1, 1), (0, 2), (1, 2)))
    GROUPS = (0, 1, 1, 2, 2, 3, 3) + (4,) * 8
    gathers = []
    gathered = []

    def gather(buffer, pieces, sender):
        width = buffer.shape[1] // pieces
        for p in range(pieces):
            copies = []
            for kind, ((fh, dy), to) in enumerate(KINDS):
                owner = real_of(fh, dy, 0)
                block = buffer.at[pl.ds(pl.multiple_of(owner * rows, rows), rows), pl.ds(p * width, width)]
                index = len(gathers) * 5 + GROUPS[kind]
                copies.append(
                    pltpu.make_async_remote_copy(
                        src_ref=block, dst_ref=block, send_sem=sent.at[sender], recv_sem=ar.at[index],
                        device_id=(real_of(*to), site), device_id_type=MESH,
                    )
                )
            gathers.append(copies)
            gathered.append((buffer, width))

    gather(gv, QUARTERS, 1)
    gather(gu, HALVES, 2)
    ua, ub = QUARTERS, QUARTERS + 1

    def start(piece, *kinds):
        for kind in kinds:
            gathers[piece][kind].start()

    def step(piece, number):
        buffer, width = gathered[piece]
        if number > 0:
            blocks = (1, 2, 2, 2, 8)[number - 1]
            take(ar.at[piece * 5 + number - 1], buffer.at[pl.ds(0, blocks * rows), pl.ds(0, width)])
        start(piece, *((0, 1, 2, 7), (3, 4, 8), (5, 9, 10), (6, 12, 11), (13, 14), ())[number])

    def steps(*numbers):
        for quarter, number in numbers:
            step(quarter, number)

    def noise_copy(c, way, hop):
        return pltpu.make_async_remote_copy(
            src_ref=nt.at[0 if hop == 0 else AT[-way], part(c)],
            dst_ref=nt.at[AT[-way * (hop + 1)], part(c)],
            send_sem=sent.at[3], recv_sem=nr.at[c * 2 + hop],
            device_id=(real, site_of(0, way)), device_id_type=MESH,
        )

    noise_copies = {(c, way, hop): noise_copy(c, way, hop) for c in range(len(CHUNKS)) for way in (1, -1) for hop in (0, 1)}

    def turn(c):
        noise_loads[c].wait()
        nt[0, part(c), :] = noise[:, part(c)].T

    def first(c):
        for way in (1, -1):
            noise_copies[c, way, 0].start()

    def forward(c):
        take(nr.at[c * 2], nt.at[pl.ds(1, 2), part(c)])
        for way in (1, -1):
            noise_copies[c, way, 1].start()

    def far(c):
        take(nr.at[c * 2 + 1], nt.at[pl.ds(3, 2), part(c)])

    def coef_copy(m, c):
        dj, fx, di = SLOTS[m]
        return pltpu.make_async_remote_copy(
            src_ref=cs.at[part(c), fixed(m)], dst_ref=cr.at[part(c), fixed(m)],
            send_sem=sent.at[4], recv_sem=pr.at[c * 4 + sum(m >= first for first in LATE[:3])],
            device_id=(real, site_of(fx, di)), device_id_type=MESH,
        )

    coef_copies = {(m, c): coef_copy(m, c) for m in range(SENT) for c in range(len(CHUNKS))}
    level = lax.broadcasted_iota(jnp.int32, (1, unit), 1) // rank_block

    def project(m, c):
        dj, fx, di = SLOTS[m]
        projected = jnp.dot(nt[AT[dj], part(c), :], gv[:, fixed(m)], preferred_element_type=jnp.float32)
        alive = (level < ranks[site_of(fx, di), site_of(0, dj)]).astype(jnp.float32)
        (cs if m < SENT else cr)[part(c), fixed(m)] = (projected * alive).astype(jnp.bfloat16)

    def projects(c, *slots):
        waiting = None
        for m in slots:
            project(m, c)
            if waiting is not None:
                coef_copies[waiting, c].start()
            waiting = m if m < SENT else None
        if waiting is not None:
            coef_copies[waiting, c].start()

    def dot_t(left, right):
        return lax.dot_general(left, right, (((1,), (1,)), ((), ())), preferred_element_type=jnp.float32)

    block = 512

    def product(here, c, lo, hi):
        span = pl.ds(lo * unit, (hi - lo) * unit)
        return dot_t(gu[here, span], cr[part(c), span])

    def blocks():
        return pl.loop(0, out.shape[0] // block)

    def rows_of(k):
        return pl.ds(pl.multiple_of(k * block, block), block)

    def early(c):
        @blocks()
        def _(k):
            out[rows_of(k), part(c)] = product(rows_of(k), c, *EARLY[0]) + product(rows_of(k), c, *EARLY[1])

    def middle(c, group):
        @blocks()
        def _(k):
            out[rows_of(k), part(c)] += product(rows_of(k), c, LATE[group], LATE[group + 1])

    def late(c, start_slot, end):
        begin, width = CHUNKS[c]

        @blocks()
        def _(k):
            here = rows_of(k)
            total = out[here, part(c)] + product(here, c, start_slot, end)
            shape = gb[here, :], ib[here, :], hb[here, :]
            for q in range(0, width, 128):
                out[here, pl.ds(begin + q, 128)] = tukey(total[:, q:q + 128], *shape)

    def arrived(c, *groups):
        for group in groups:
            slots = LATE[0] if group < 0 else LATE[group + 1] - LATE[group]
            take(pr.at[c * 4 + group + 1], cr.at[part(c), pl.ds(0, slots * unit)])

    pl.semaphore_wait(barrier, len(peers))
    for m in v_copies:
        v_copies[m].start()
    turn(0)
    turn(1)
    first(0)
    turn(2)
    first(1)
    take(local.at[6], gv.at[pl.ds(0, rows), pl.ds(0, len(resident) * unit)])
    take(local.at[7], gu.at[pl.ds(0, rows), :])
    for copy in small_loads:
        copy.wait()
    for k in range(skew.shape[0]):
        spread = pl.ds(k * 128, 128)
        gb[spread, :] = jnp.broadcast_to(skew[pl.ds(k, 1), :], (128, 128)).T
        ib[spread, :] = 1.0 / gb[spread, :]
        hb[spread, :] = 0.5 * jnp.broadcast_to(tail[pl.ds(k, 1), :], (128, 128)).T

    def ready(quarter):
        count = len(SLOTS) // QUARTERS
        coming = sum(m in v_copies for m in range(quarter * count, (quarter + 1) * count))
        take(vr.at[quarter], gv.at[pl.ds(0, rows), pl.ds(0, coming * unit)])
        step(quarter, 0)

    ready(0)
    steps((0, 1), (0, 2))
    start(ua, 0, 7)
    steps((0, 3))
    ready(1)
    ready(2)
    steps((0, 4), (0, 5))
    projects(0, 0)
    projects(1, 0)
    projects(2, 0)
    ready(3)
    steps((1, 1), (1, 2))
    forward(0)
    projects(0, 1, 2)
    steps((2, 1), (1, 3), (2, 2), (3, 1))
    steps((1, 4), (2, 3), (3, 2))
    forward(1)
    first(2)
    projects(1, 1, 2)
    start(ub, 0, 7)
    start(ua, 1, 2)
    steps((1, 5), (2, 4), (3, 3))
    far(0)
    projects(0, 3, 4)
    steps((2, 5), (3, 4), (3, 5))
    step(ua, 1)
    start(ub, 1, 2)
    projects(0, 9, 10, 7, 8)
    far(1)
    projects(1, 3, 4)
    step(ua, 2)
    projects(0, 11, 12, 13, 14, 15)
    projects(1, 11, 12, 13, 14, 15)
    step(ua, 3)
    step(ub, 1)
    forward(2)
    projects(0, 5, 6)
    projects(1, 9, 10, 7, 8, 5, 6)
    projects(2, 1, 2)
    projects(2, 11, 12, 13)
    step(ua, 4)
    step(ub, 2)
    far(2)
    projects(2, 3, 4, 9, 10, 5, 6, 7, 8)
    step(ub, 3)
    step(ub, 4)
    step(ua, 5)
    step(ub, 5)
    projects(2, 14, 15)
    arrived(0, -1)
    early(0)
    arrived(0, 0, 1, 2)
    late(0, LATE[0], LATE[3])
    arrived(1, -1)
    early(1)
    arrived(2, -1)
    early(2)
    arrived(1, 0, 1, 2)
    late(1, LATE[0], LATE[3])
    arrived(2, 2)
    middle(2, 2)
    arrived(2, 0)
    middle(2, 0)
    arrived(2, 1)
    late(2, LATE[1], LATE[2])

    take(sent.at[0], gv.at[pl.ds(0, rows), pl.ds(0, len(v_copies) * unit)])
    take(sent.at[1], gv.at[pl.ds(0, 15 * rows), :])
    take(sent.at[2], gu.at[pl.ds(0, 15 * rows), :])
    take(sent.at[3], nt.at[pl.ds(0, 4)])
    take(sent.at[4], cs)


def per_device(noise, v_factors, u_factors, ranks, skew_g, tail_h):
    v, u = v_factors[0], u_factors[0]
    tile, count = noise.shape
    columns = v.shape[1]
    anywhere = pl.BlockSpec(memory_space=pl.ANY)
    dma = pltpu.SemaphoreType.DMA
    skew, tail = skew_g.reshape(-1, 128), tail_h.reshape(-1, 128)
    return pl.pallas_call(
        kernel,
        out_shape=pltpu.VMEM((tile, count), jnp.float32),
        in_specs=[anywhere] * 6,
        out_specs=pl.BlockSpec(memory_space=pltpu.VMEM),
        scratch_shapes=[
            pltpu.VMEM((tile, count), jnp.bfloat16),
            pltpu.SMEM(ranks.shape, jnp.int32),
            pltpu.VMEM(skew.shape, jnp.float32),
            pltpu.VMEM(tail.shape, jnp.float32),
            pltpu.VMEM((5, count, tile), jnp.bfloat16),
            pltpu.VMEM((tile, columns), jnp.bfloat16),
            pltpu.VMEM((tile, columns), jnp.bfloat16),
            pltpu.VMEM((count, columns // len(SLOTS) * SENT), jnp.bfloat16),
            pltpu.VMEM((count, columns), jnp.bfloat16),
            pltpu.VMEM((tile, 128), jnp.float32),
            pltpu.VMEM((tile, 128), jnp.float32),
            pltpu.VMEM((tile, 128), jnp.float32),
            dma((5,)),
            dma((QUARTERS,)),
            dma(((QUARTERS + HALVES) * 5,)),
            dma((2 * len(CHUNKS),)),
            dma((4 * len(CHUNKS),)),
            dma((8,)),
        ],
        compiler_params=pltpu.CompilerParams(
            collective_id=0, has_side_effects=True, vmem_limit_bytes=60 * 1024 * 1024
        ),
    )(noise, v, u, ranks, skew, tail)


def solution(mesh):
    placed = (
        P("site", "real"),
        P("site", "real", None),
        P("site", "real", None),
        P(),
        P("site"),
        P("site"),
    )
    return jax.shard_map(
        per_device, mesh=mesh, in_specs=placed, out_specs=P("site", "real"), check_vma=False
    )
```
